512 devices in a mesh: expert: 64 (over z, y), tensor: 8 (over x, core).
Axes of the slice: x: 4, y: 8, z: 8, core: 2. Of those that a mesh axis runs over, the one named last changes fastest.
Arguments:
- attn_out: bfloat16 [8192, 4096], P('expert', 'tensor'), may hold values from -6 to 6
- out_weight: bfloat16 [4096, 2048], P('tensor'), may hold values from -0.09375 to 0.09375
- residual: bfloat16 [8192, 2048], P(('expert', 'tensor')), may hold values from -6 to 6
- attn_gain: float32 [2048], replicated, may hold values from 0.1 to 1.9
- expert_ids: int32 [8192, 8], P('expert'), may hold values from 0 to 127, all different within a row; in each aligned block of 128 rows (0 to 127, 128 to 255, ...) at most 12 rows name the same one
- route_weights: float32 [8192, 8], P('expert'), may hold values from 0.05 to 0.3
- w_gate: bfloat16 [64, 2048, 1536], P('expert', None, 'tensor'), may hold values from -0.125 to 0.125
- w_up: bfloat16 [64, 2048, 1536], P('expert', None, 'tensor'), may hold values from -0.125 to 0.125
- w_down: bfloat16 [64, 1536, 2048], P('expert', 'tensor'), may hold values from -0.21875 to 0.21875
- input_gain: float32 [2048], replicated, may hold values from 0.1 to 1.9
- q_weight: bfloat16 [2048, 4096], P('expert', 'tensor'), may hold values from -0.125 to 0.125
- kv_weight: bfloat16 [2048, 1024], P('expert', 'tensor'), may hold values from -0.125 to 0.125
- q_gain: float32 [128], replicated, may hold values from 0.1 to 1.9
- k_gain: float32 [128], replicated, may hold values from 0.1 to 1.9
Outputs:
- next_residual: bfloat16 [8192, 2048], P(('expert', 'tensor'))
- queries: bfloat16 [8192, 4096], P('expert', 'tensor')
- keys_values: bfloat16 [8192, 1024], P('expert', 'tensor')
The draws below stay inside these ranges and needn't reach their ends.
Inputs may be any that keep to these rules, and one draw needn't show every extreme that they name: `expert_ids`: each row names 8 different experts. In each aligned block of 128 rows no expert is named by more than 12 rows, and in some block one expert is named by exactly 12 rows.
All inputs are finite; a program needn't handle non-finite values.
Results may differ from the reference program's by a relative error of at most 0.012.
Values may be sent and summed in bfloat16 or wider, within the bound.
A program may use at most 64 MiB of HBM per device.

```python
import math
import jax
import jax.numpy as jnp
import numpy as np
from jax import lax

D = 2048
FF = 768
HEADS = 32
KV_HEADS = 4
HEAD_DIM = 128
TOP = 8
EXPERTS = 128
GROUP = 128
TOKENS = 8192
CAP = 12
SHARE = 4
FF_DEV = 192
N_EXPERT = 64


def levels(stream_key, dims, pieces, low, top_value):
    level, own = 1.0, jax.random.fold_in(stream_key, 6)
    for position, blocks in pieces:
        heights = jnp.exp(jax.random.uniform(jax.random.fold_in(own, position), (blocks,), jnp.float32, low / len(pieces), top_value / len(pieces)))
        level = level * jnp.repeat(heights, dims[position] // blocks).reshape([-1 if axis == position else 1 for axis in range(len(dims))])
    return level


def shared_out(stream_key, own, number, rows, count, top, most, slope):
    ranking = jax.random.permutation(stream_key, count)
    packed, usual = load_shares(count, rows * top, most, slope, True), load_shares(count, rows * top, most, slope, False)
    places = jnp.arange(count)

    def named(tallies, offset_by):
        used = int((tallies > 0).sum())
        fixed = max(1, used // 4)
        shifted = fixed + (places - fixed + offset_by * (used - fixed)) % max(1, count - fixed)
        return jnp.zeros((count,), jnp.int32).at[ranking[jnp.where(places < fixed, places, shifted)]].set(jnp.asarray(tallies, jnp.int32))

    tallies = jnp.where(number % 4 == 0, named(packed, number // 4), named(usual, number - number // 4 - 1))
    mixed = jax.random.permutation(jax.random.fold_in(own, 3), count)
    donor, receiver = mixed[0:count // 2 * 2:2], mixed[1:count // 2 * 2:2]
    margin = jnp.minimum(tallies[donor] - 1, most - tallies[receiver]) // 2
    margin = jnp.where((donor == ranking[0]) | (receiver == ranking[0]) | (tallies[receiver] == 0), 0, jnp.maximum(margin, 0))
    shifted = jax.random.randint(jax.random.fold_in(own, 4), (count // 2,), 0, 1 << 20) % (margin + 1)
    tallies = tallies.at[donor].add(-shifted).at[receiver].add(shifted)
    labels = jnp.searchsorted(jnp.cumsum(tallies), jnp.arange(rows * top), side="right").astype(jnp.int32)
    listing = labels.reshape(top, rows).T
    listing = listing[jax.random.permutation(jax.random.fold_in(own, 1), rows)]
    offset_by = jax.random.randint(jax.random.fold_in(own, 2), (rows, 1), 0, top)
    return jnp.take_along_axis(listing, (jnp.arange(top)[None, :] + offset_by) % top, axis=1)


def load_shares(count, total, most, slope, full):
    portions = [(1 << 20) // math.isqrt(rank ** slope) + 1 for rank in range(1, count + 1)]
    largest = most if full else min(most, max(-(-total // count), total * portions[0] // sum(portions)))
    least = 1 if total - largest >= count - 1 else 0
    holding, spare = [largest] + [least] * (count - 1), total - largest - least * (count - 1)
    while spare > 0:
        movable = [i for i in range(1, count) if holding[i] < largest] or [i for i in range(1, count) if holding[i] < most]
        pool, left = sum([portions[i] for i in movable]), spare
        for i in movable:
            extra = min(most - holding[i], max(1, left * portions[i] // pool), spare)
            holding[i] = holding[i] + extra
            spare = spare - extra
    return np.array(holding)


def centred(stream_key, shape, deviation, bound, cuts=(), kind=jnp.bfloat16):
    array = deviation * jax.random.normal(stream_key, shape, jnp.float32)
    if cuts:
        array = array * levels(stream_key, shape, cuts, -0.22, 0.18)
    return jnp.clip(array, -bound, bound).astype(kind)


def setup_inputs(seed: int = 0) -> dict:
    streams_of = jax.random.split(jax.random.key(seed), 15)
    attn_out = centred(streams_of[0], (TOKENS, HEADS * HEAD_DIM), 1.0, 6.0, ((0, 64), (1, 8)))
    out_weight = centred(streams_of[1], (HEADS * HEAD_DIM, D), (HEADS * HEAD_DIM) ** -0.5, 0.09375, ((0, 8),))
    residual = centred(streams_of[2], (TOKENS, D), 1.0, 6.0, ((0, 512),))
    attn_gain = jnp.clip(1.0 + 0.18 * jax.random.normal(streams_of[3], (D,), jnp.float32), 0.1, 1.9)
    expert_ids_keys = jax.random.split(jax.random.fold_in(streams_of[4], 1), TOKENS // GROUP)
    expert_ids_turns = jax.random.permutation(jax.random.fold_in(streams_of[4], 3), TOKENS // GROUP)
    expert_ids = jax.vmap(lambda own, number: shared_out(jax.random.fold_in(streams_of[4], 2), own, number, GROUP, EXPERTS, TOP, CAP, 2))(expert_ids_keys, expert_ids_turns).reshape((TOKENS, TOP))
    route_weights = jnp.clip(0.05 + 0.25 * jax.random.uniform(streams_of[5], (TOKENS, TOP), jnp.float32) ** levels(streams_of[5], (TOKENS, TOP), ((0, 64),), -0.2, 0.2), 0.05, 0.3)
    w_gate = centred(streams_of[6], (EXPERTS // 2, D, 2 * FF), D ** -0.5, 0.125, ((0, 64), (2, 8)))
    w_up = centred(streams_of[7], (EXPERTS // 2, D, 2 * FF), D ** -0.5, 0.125, ((0, 64), (2, 8)))
    w_down = centred(streams_of[8], (EXPERTS // 2, 2 * FF, D), FF ** -0.5, 0.21875, ((0, 64), (1, 8)))
    input_gain = jnp.clip(1.0 + 0.18 * jax.random.normal(streams_of[9], (D,), jnp.float32), 0.1, 1.9)
    q_weight = centred(streams_of[10], (D, HEADS * HEAD_DIM), D ** -0.5, 0.125, ((0, 64), (1, 8)))
    kv_weight = centred(streams_of[11], (D, 2 * KV_HEADS * HEAD_DIM), D ** -0.5, 0.125, ((0, 64), (1, 8)))
    q_gain = jnp.clip(1.0 + 0.18 * jax.random.normal(streams_of[12], (HEAD_DIM,), jnp.float32), 0.1, 1.9)
    k_gain = jnp.clip(1.0 + 0.18 * jax.random.normal(streams_of[13], (HEAD_DIM,), jnp.float32), 0.1, 1.9)
    return dict(attn_out=attn_out, out_weight=out_weight, residual=residual, attn_gain=attn_gain, expert_ids=expert_ids, route_weights=route_weights, w_gate=w_gate, w_up=w_up, w_down=w_down, input_gain=input_gain, q_weight=q_weight, kv_weight=kv_weight, q_gain=q_gain, k_gain=k_gain)


EPSILON = 1e-06

def normalize(values, gain):
    return values * lax.rsqrt(lax.optimization_barrier(jnp.mean(values * values, axis=-1, keepdims=True)) + EPSILON) * gain

def block_slots(ids_block, weight_block, base):
    flat = ids_block.reshape(-1)
    onehot = (flat[:, None] == jnp.arange(EXPERTS, dtype=jnp.int32)[None, :]).astype(jnp.int32)
    earlier = (jnp.cumsum(onehot, axis=0) - onehot).astype(jnp.int32)
    rank = lax.optimization_barrier(jnp.sum(earlier * onehot, axis=1)).astype(jnp.int32)
    dest = (flat * CAP + rank).astype(jnp.int32)
    rows = (base + jnp.arange(GROUP * TOP, dtype=jnp.int32) // TOP).astype(jnp.int32)
    slot_row = jnp.full((EXPERTS * CAP,), TOKENS, jnp.int32).at[dest].set(rows)
    slot_weight = jnp.zeros((EXPERTS * CAP,), jnp.float32).at[dest].set(weight_block.reshape(-1))
    return (slot_row, slot_weight)

def reference(attn_out, out_weight, residual, attn_gain, expert_ids, route_weights, w_gate, w_up, w_down, input_gain, q_weight, kv_weight, q_gain, k_gain):
    attn = jnp.dot(attn_out, out_weight, preferred_element_type=jnp.float32)
    first_residual = (residual.astype(jnp.float32) + attn).astype(jnp.bfloat16)
    normed = normalize(first_residual.astype(jnp.float32), attn_gain).astype(jnp.bfloat16)
    bases = (jnp.arange(N_EXPERT, dtype=jnp.int32) * GROUP).astype(jnp.int32)
    slot_row, slot_weight = jax.vmap(block_slots)(expert_ids.reshape(N_EXPERT, GROUP, TOP), route_weights.reshape(N_EXPERT, GROUP, TOP), bases)
    slot_row = jnp.transpose(slot_row.reshape(N_EXPERT, EXPERTS, CAP), (1, 0, 2)).reshape(EXPERTS, N_EXPERT * CAP)
    slot_weight = jnp.transpose(slot_weight.reshape(N_EXPERT, EXPERTS, CAP), (1, 0, 2)).reshape(EXPERTS, N_EXPERT * CAP)
    padded = jnp.concatenate([normed, jnp.zeros((1, D), jnp.bfloat16)], axis=0)
    zero = jnp.zeros((), jnp.int32)

    def one_expert(total, inputs):
        index, rows_index, weights = inputs
        pair = (index // 2).astype(jnp.int32)
        side = (index % 2).astype(jnp.int32)
        gate_w = lax.dynamic_slice(w_gate, (pair, zero, (side * FF).astype(jnp.int32)), (1, D, FF))[0]
        up_w = lax.dynamic_slice(w_up, (pair, zero, (side * FF).astype(jnp.int32)), (1, D, FF))[0]
        down_w = lax.dynamic_slice(w_down, (pair, (side * FF).astype(jnp.int32), zero), (1, FF, D))[0]
        rows = jnp.take(padded, rows_index, axis=0)
        gate = jnp.dot(rows, gate_w, preferred_element_type=jnp.float32)
        up = jnp.dot(rows, up_w, preferred_element_type=jnp.float32)
        act = (jax.nn.silu(gate) * up).astype(jnp.bfloat16)
        act_groups = act.reshape(-1, SHARE, FF_DEV).astype(jnp.float32)
        down_groups = down_w.reshape(SHARE, FF_DEV, D).astype(jnp.float32)
        parts = jnp.einsum('nsf,sfd->nsd', act_groups, down_groups).astype(jnp.bfloat16)
        summed = lax.optimization_barrier(jnp.sum(parts.astype(jnp.float32), axis=1))
        total = total.at[rows_index].add(weights[:, None] * summed)
        return (total, None)
    start = jnp.zeros((TOKENS + 1, D), jnp.float32)
    moe, unused = lax.scan(one_expert, start, (jnp.arange(EXPERTS, dtype=jnp.int32), slot_row, slot_weight))
    moe = moe[:TOKENS]
    next_residual = (first_residual.astype(jnp.float32) + moe).astype(jnp.bfloat16)
    next_normed = normalize(next_residual.astype(jnp.float32), input_gain).astype(jnp.bfloat16)
    query_raw = jnp.dot(next_normed, q_weight, preferred_element_type=jnp.float32)
    queries = normalize(query_raw.reshape(TOKENS, HEADS, HEAD_DIM), q_gain).reshape(TOKENS, HEADS * HEAD_DIM).astype(jnp.bfloat16)
    kv_raw = jnp.dot(next_normed, kv_weight, preferred_element_type=jnp.float32)
    keys = normalize(kv_raw[:, :KV_HEADS * HEAD_DIM].reshape(TOKENS, KV_HEADS, HEAD_DIM), k_gain).reshape(TOKENS, KV_HEADS * HEAD_DIM)
    keys_values = jnp.concatenate([keys, kv_raw[:, KV_HEADS * HEAD_DIM:]], axis=1).astype(jnp.bfloat16)
    return (next_residual, queries, keys_values)
```

```python
import jax
import jax.numpy as jnp
from jax import lax
from jax.experimental import pallas as pl
from jax.experimental.pallas import tpu as pltpu
from jax.sharding import PartitionSpec as P

MESH = pl.DeviceIdType.MESH
BF = jnp.bfloat16
F32 = jnp.float32

KV_HEADS = 4
TOP = 8
EPSILON = 1e-06

D = 2048
GROUP = 128
TOKENS = 16
CAP = 12
QUARTER = 512
HIDDEN = 192
PAIR_HIDDEN = 384
ROWS = 384
SLOTS = 768
QKV = 640
HEAD = 128


def normalize(values, gain):
    return values * lax.rsqrt(jnp.mean(values * values, axis=-1, keepdims=True) + EPSILON) * gain


def dot(a, b):
    return jnp.dot(a, b, preferred_element_type=F32)


def iota(shape, axis):
    return lax.broadcasted_iota(jnp.int32, shape, axis)


def kernel(
    attn_hbm,
    ow_hbm,
    res_ref,
    attn_gain,
    ids_ref,
    rw_ref,
    wg_hbm,
    wu_hbm,
    wd_hbm,
    input_gain,
    qw_hbm,
    kvw_hbm,
    q_gain,
    k_gain,
    next_ref,
    queries_ref,
    kv_ref,
    attn,
    ow,
    wg,
    wu,
    wgp,
    wup,
    wgu,
    wd_own,
    wd,
    qw,
    partial,
    rs_in,
    normed_out,
    normed_in,
    pick,
    mix_hi,
    mix_lo,
    tx,
    r1,
    x0,
    x1,
    c0,
    c1,
    hidden,
    act,
    act_in,
    y_acc,
    y0,
    y1,
    r3,
    r4,
    sums_out,
    sums_in,
    first,
    nx,
    load_sem,
    rs_send,
    rs_recv,
    nb_send,
    nb_recv,
    pair_send,
    pair_recv,
    wd_send,
    wd_recv,
    q1_send,
    q1_recv,
    q2_send,
    q2_recv,
    d1_send,
    d1_recv,
    d2_send,
    d2_recv0,
    d2_recv1,
    c_send,
    c_recv0,
    c_recv1,
    act_send,
    act_recv,
    r3_send,
    r3_recv,
    r4_send,
    r4_recv,
    sums_send,
    sums_recv,
    nx_send,
    nx_recv,
):
    e = lax.axis_index("expert")
    t = lax.axis_index("tensor")
    z, y = e // 8, e % 8
    core = t % 2
    side = (t // 2) % 2
    parity = t // 4
    partner = t + 1 - 2 * core
    cross = t + 2 - 4 * side
    core0, core1 = t - core, t - core + 1
    half = z // 4
    a = y + core * (z - y)
    b = z + core * (y - z)

    def at(first_axis, second_axis):
        return (second_axis + core * (first_axis - second_axis)) * 8 + (
            first_axis + core * (second_axis - first_axis)
        )

    def step_of(i):
        return jnp.where(i % 2 == 1, (i + 1) // 2, 8 - i // 2)

    def remote(src, dst, send, recv, expert, tensor):
        return pltpu.make_async_remote_copy(
            src_ref=src,
            dst_ref=dst,
            send_sem=send,
            recv_sem=recv,
            device_id={"expert": expert, "tensor": tensor},
            device_id_type=MESH,
        )

    def arrived(dst, send, recv):
        remote(dst, dst, send, recv, e, partner).wait_recv()

    def left(src, send, recv):
        remote(src, src, send, recv, e, partner).wait_send()

    barrier = pltpu.get_barrier_semaphore()

    @pl.loop(1, 8)
    def _(i):
        pl.semaphore_signal(
            barrier, inc=1, device_id={"expert": e, "tensor": (t + i) % 8}, device_id_type=MESH
        )
        for which in (core0, core1):
            pl.semaphore_signal(
                barrier,
                inc=1,
                device_id={"expert": z * 8 + (y + i) % 8, "tensor": which},
                device_id_type=MESH,
            )
            pl.semaphore_signal(
                barrier,
                inc=1,
                device_id={"expert": ((z + i) % 8) * 8 + y, "tensor": which},
                device_id_type=MESH,
            )

    loads = [
        pltpu.make_async_copy(attn_hbm, attn, load_sem.at[0]),
        pltpu.make_async_copy(ow_hbm, ow, load_sem.at[1]),
        pltpu.make_async_copy(qw_hbm, qw.at[b, a, :, pl.ds(0, 512)], load_sem.at[2]),
        pltpu.make_async_copy(kvw_hbm, qw.at[b, a, :, pl.ds(512, 128)], load_sem.at[3]),
        pltpu.make_async_copy(wg_hbm.at[0], wg, load_sem.at[4]),
        pltpu.make_async_copy(wu_hbm.at[0], wu, load_sem.at[5]),
        pltpu.make_async_copy(wd_hbm.at[0], wd_own, load_sem.at[6]),
    ]
    for load in loads:
        load.start()

    loads[0].wait()
    loads[1].wait()
    for n in range(4):
        cols = slice(n * 512, n * 512 + 512)
        partial[:, :, cols] = dot(attn[...], ow[:, cols]).astype(BF).reshape(8, TOKENS, 512)

    pl.semaphore_wait(barrier, 35)

    @pl.loop(1, 8)
    def _(i):
        d = (t + i) % 8
        remote(partial.at[d], rs_in.at[t], rs_send.at[d], rs_recv.at[t], e, d).start()

    loads[2].wait()
    loads[3].wait()

    @pl.loop(1, 8)
    def _(i):
        d = (a + step_of(i)) % 8
        remote(
            qw.at[b, a], qw.at[b, a], q1_send.at[d], q1_recv.at[a], at(d, b), t
        ).start()

    loads[4].wait()
    remote(wg, wgp, pair_send.at[0], pair_recv.at[0], e, partner).start()
    loads[5].wait()
    remote(wu, wup, pair_send.at[1], pair_recv.at[1], e, partner).start()

    position = iota((GROUP, 64), 1)
    p_first, p_second = position // 8, position % 8
    expert_of = 2 * at(p_first, p_second) + parity
    ids = ids_ref[...]
    weights = rw_ref[...]
    named = jnp.zeros((GROUP, 64), F32)
    weight_of = jnp.zeros((GROUP, 64), F32)
    for k in range(TOP):
        hit = expert_of == ids[:, k : k + 1]
        named += jnp.where(hit, 1.0, 0.0)
        weight_of += jnp.where(hit, weights[:, k : k + 1], 0.0)
    lower = jnp.where(iota((GROUP, GROUP), 1) < iota((GROUP, GROUP), 0), 1.0, 0.0).astype(BF)
    rank = dot(lower, named.astype(BF))
    code = (named * (rank + 1.0)).astype(BF)
    slot = iota((64, SLOTS), 1)
    start = iota((64, SLOTS), 0) * CAP
    spread = jnp.where((slot >= start) & (slot < start + CAP), 1.0, 0.0).astype(BF)
    wanted = (iota((GROUP, SLOTS), 1) % CAP + 1).astype(F32)
    chosen = dot(code, spread) == wanted
    high = weight_of.astype(BF)
    low = (weight_of - high.astype(F32)).astype(BF)
    mix_hi[...] = jnp.where(chosen, dot(high, spread), 0.0).astype(BF)
    mix_lo[...] = jnp.where(chosen, dot(low, spread), 0.0).astype(BF)
    pick[...] = jnp.where(chosen, 1.0, 0.0).T.astype(BF)

    after, before = at(a, (b + 1) % 8), at(a, (b + 7) % 8)

    def ring(step):
        rows = ((b + 8 - step) % 8, (b + step) % 8)
        if step == 3:
            pieces = (qw.at[rows[0], pl.ds(0, 4)], qw.at[rows[1], pl.ds(4, 4)])
        else:
            pieces = (qw.at[rows[0]], qw.at[rows[1]])
        return [
            remote(pieces[k], pieces[k], q2_send.at[step, k], q2_recv.at[step, k], (after, before)[k], t)
            for k in range(2)
        ]

    def ring_wait(step):
        rows = ((b + 7 - step) % 8, (b + 1 + step) % 8)
        if step == 3:
            pieces = (qw.at[rows[0], pl.ds(0, 4)], qw.at[rows[1], pl.ds(4, 4)])
        else:
            pieces = (qw.at[rows[0]], qw.at[rows[1]])
        for k in range(2):
            arrived(pieces[k], q2_send.at[step, k], q2_recv.at[step, k])

    @pl.loop(1, 8)
    def _(i):
        s = (a + i) % 8
        arrived(qw.at[b, s], q1_send.at[s], q1_recv.at[s])

    for c in ring(0):
        c.start()

    rs_in[t] = partial[t]

    @pl.loop(1, 8)
    def _(i):
        s = (t + i) % 8
        arrived(rs_in.at[s], rs_send.at[s], rs_recv.at[s])

    total = res_ref[...].astype(F32)
    attn_sum = rs_in[0].astype(F32)
    for k in range(1, 8):
        attn_sum += rs_in[k].astype(F32)
    first_residual = (total + attn_sum).astype(BF)
    first[...] = first_residual
    normed = normalize(first_residual.astype(F32), attn_gain[...]).astype(BF)
    for s in range(4):
        normed_out[s] = normed[:, s * QUARTER : s * QUARTER + QUARTER]
    normed_in[t] = normed_out[t % 4]

    @pl.loop(1, 8)
    def _(i):
        d = (t + i) % 8
        remote(normed_out.at[d % 4], normed_in.at[t], nb_send.at[d], nb_recv.at[t], e, d).start()

    loads[6].wait()
    own_half = pl.ds(pl.multiple_of(side * 1024, 1024), 1024)
    other_half = pl.ds(pl.multiple_of((1 - side) * 1024, 1024), 1024)
    remote(wd_own.at[:, own_half], wd.at[1], wd_send.at[0], wd_recv.at[0], e, partner).start()
    remote(wd_own.at[:, other_half], wd.at[2], wd_send.at[1], wd_recv.at[1], e, cross).start()
    wd[0] = wd_own[:, own_half]

    ring_wait(0)
    for c in ring(1):
        c.start()

    @pl.loop(1, 8)
    def _(i):
        s = (t + i) % 8
        arrived(normed_in.at[s], nb_send.at[s], nb_recv.at[s])

    group = normed_in[...].reshape(GROUP, QUARTER)
    for k in range(4):
        rows = slice(k * 192, k * 192 + 192)
        tx[2 * k : 2 * k + 2] = (
            dot(pick[rows, :], group).astype(BF).reshape(2, 8, 3, 4, QUARTER)
        )

    @pl.loop(1, 8)
    def _(i):
        d = (a + step_of(i)) % 8
        remote(tx.at[d], r1.at[a], d1_send, d1_recv, at(d, b), t).start()

    keep = pltpu.make_async_copy(tx.at[a], r1.at[a], d1_recv)
    keep.start()

    arrived(wgp, pair_send.at[0], pair_recv.at[0])
    arrived(wup, pair_send.at[1], pair_recv.at[1])

    @pl.loop(0, 16)
    def _(i):
        rows = pl.ds(pl.multiple_of(i * 128, 128), 128)
        wgu[rows, 0:PAIR_HIDDEN] = jnp.concatenate([wg[rows, :], wgp[rows, :]], axis=1)
        wgu[rows, PAIR_HIDDEN : 2 * PAIR_HIDDEN] = jnp.concatenate(
            [wu[rows, :], wup[rows, :]], axis=1
        )

    arrived(wd.at[2], wd_send.at[1], wd_recv.at[1])
    remote(wd.at[2], wd.at[3], wd_send.at[2], wd_recv.at[2], e, partner).start()

    arrived(r1, d1_send, d1_recv)

    def to_core0_path(d):
        return r1.at[:, d], x0.at[z % 4], d2_recv0.at[z % 4]

    def to_core1_path(d, hf):
        return r1.at[4 * hf : 4 * hf + 4, d], x1.at[y], d2_recv1.at[y]

    @pl.when(core == 0)
    def _():
        @pl.loop(1, 8)
        def _(i):
            d = (b + step_of(i)) % 8
            src, dst, sem = to_core0_path(d)
            remote(src, dst, d2_send, sem, at(a, d), core0 + half).start()

        src, dst, sem = to_core0_path(b)

        @pl.when(half == 0)
        def _():
            pltpu.make_async_copy(src, dst, sem).start()

        @pl.when(half == 1)
        def _():
            remote(src, dst, d2_send, sem, e, core1).start()

    @pl.when(core == 1)
    def _():
        @pl.loop(1, 8)
        def _(i):
            d = (b + step_of(i)) % 8
            for hf in range(2):
                src, dst, sem = to_core1_path(d, hf)
                remote(src, dst, d2_send, sem, at(a, d), core0 + hf).start()

        src, dst, sem = to_core1_path(b, 0)
        remote(src, dst, d2_send, sem, e, core0).start()
        src, dst, sem = to_core1_path(b, 1)
        pltpu.make_async_copy(src, dst, sem).start()

    @pl.loop(0, 4)
    def _(i):
        for j in range(2):
            k = (y + step_of(2 * i + j)) % 8
            arrived(x1.at[k], c_send, d2_recv1.at[k])
            remote(x1.at[k], c1.at[k], c_send, c_recv1.at[k], e, cross).start()
        arrived(x0.at[i], c_send, d2_recv0.at[i])
        remote(x0.at[i], c0.at[i], c_send, c_recv0.at[i], e, cross).start()

    ring_wait(1)
    for c in ring(2):
        c.start()

    def multiply(rows_of, column, zero):
        rows = pl.ds(pl.multiple_of(column, QUARTER), QUARTER)
        values = rows_of()
        for n in range(3):
            cols = slice(n * 256, n * 256 + 256)
            product = dot(values, wgu[rows, cols])
            hidden[:, cols] = product if zero else hidden[:, cols] + product

    def natural(ref):
        return lambda: ref[...].reshape(ROWS, QUARTER)

    def turned(ref):
        return lambda: jnp.concatenate(
            [ref[:, k].reshape(96, QUARTER) for k in range(4)], axis=0
        )

    multiply(natural(x0), side * 1024, True)
    multiply(turned(x1), side * 1024 + QUARTER, False)

    @pl.loop(0, 4)
    def _(i):
        arrived(c0.at[i], c_send, c_recv0.at[i])

    multiply(natural(c0), (1 - side) * 1024, False)

    @pl.loop(0, 8)
    def _(i):
        arrived(c1.at[i], c_send, c_recv1.at[i])

    multiply(turned(c1), (1 - side) * 1024 + QUARTER, False)

    gate = hidden[:, 0:PAIR_HIDDEN]
    act[...] = (
        gate * (1.0 / (1.0 + jnp.exp(-gate))) * hidden[:, PAIR_HIDDEN : 2 * PAIR_HIDDEN]
    ).astype(BF)
    remote(act, act_in, act_send, act_recv, e, cross).start()

    ring_wait(2)
    for c in ring(3):
        c.start()

    arrived(wd.at[1], wd_send.at[0], wd_recv.at[0])
    arrived(wd.at[3], wd_send.at[2], wd_recv.at[2])
    for n in range(4):
        cols = slice(n * 256, n * 256 + 256)
        y_acc[:, cols] = dot(act[...], wd[0:2, :, cols].reshape(PAIR_HIDDEN, 256))
    arrived(act_in, act_send, act_recv)
    for n in range(4):
        cols = slice(n * 256, n * 256 + 256)
        out = y_acc[:, cols] + dot(act_in[...], wd[2:4, :, cols].reshape(PAIR_HIDDEN, 256))
        blocks = out.astype(BF).reshape(4, 8, 3, 4, 256)
        into = slice((n % 2) * 256, (n % 2) * 256 + 256)
        if n < 2:
            y0[:, :, :, :, into] = blocks
        else:
            for k in range(4):
                y1[:, k, :, :, into] = blocks[k]

    first_zone = 4 * core

    @pl.loop(0, 4)
    def _(i):
        zone = first_zone + i
        src, dst = y0.at[i], r3.at[z]

        @pl.when(zone != z)
        def _():
            remote(src, dst, r3_send, r3_recv, zone * 8 + y, core0).start()

        @pl.when((zone == z) & (core == 0))
        def _():
            pltpu.make_async_copy(src, dst, r3_recv).start()

        @pl.when((zone == z) & (core == 1))
        def _():
            remote(src, dst, r3_send, r3_recv, e, core0).start()

    @pl.loop(1, 8)
    def _(i):
        d = (y + step_of(i)) % 8
        remote(
            y1.at[d], r3.at[y, pl.ds(first_zone, 4)], r3_send, r3_recv, z * 8 + d, core1
        ).start()

    @pl.when(core == 1)
    def _():
        pltpu.make_async_copy(y1.at[y], r3.at[y, pl.ds(first_zone, 4)], r3_recv).start()

    @pl.when(core == 0)
    def _():
        remote(y1.at[y], r3.at[y, pl.ds(first_zone, 4)], r3_send, r3_recv, e, core1).start()

    arrived(r3, r3_send, r3_recv)

    @pl.loop(1, 8)
    def _(i):
        d = (a + step_of(i)) % 8
        remote(r3.at[:, d], r4.at[a], r4_send, r4_recv, at(d, b), t).start()

    pltpu.make_async_copy(r3.at[:, a], r4.at[a], r4_recv).start()
    arrived(r4, r4_send, r4_recv)

    returned = r4[...].reshape(SLOTS, QUARTER)
    weighted = dot(mix_hi[...], returned) + dot(mix_lo[...], returned)
    sums_out[...] = weighted.astype(BF).reshape(8, TOKENS, QUARTER)
    sums_in[t] = sums_out[t]

    @pl.loop(1, 8)
    def _(i):
        d = (t + i) % 8
        remote(sums_out.at[d], sums_in.at[t], sums_send.at[d], sums_recv.at[t], e, d).start()

    @pl.loop(1, 8)
    def _(i):
        s = (t + i) % 8
        arrived(sums_in.at[s], sums_send.at[s], sums_recv.at[s])

    expert_sum = jnp.concatenate(
        [sums_in[s].astype(F32) + sums_in[s + 4].astype(F32) for s in range(4)], axis=1
    )
    next_residual = (first[...].astype(F32) + expert_sum).astype(BF)
    next_ref[...] = next_residual
    nx[t] = normalize(next_residual.astype(F32), input_gain[...]).astype(BF)

    @pl.loop(1, 8)
    def _(i):
        d = (t + i) % 8
        remote(nx.at[t], nx.at[t], nx_send.at[d], nx_recv.at[t], e, d).start()

    ring_wait(3)

    @pl.loop(1, 8)
    def _(i):
        s = (t + i) % 8
        arrived(nx.at[s], nx_send.at[s], nx_recv.at[s])

    tokens = nx[...].reshape(GROUP, D)
    raw = jnp.zeros((GROUP, QKV), F32)
    for zz in range(8):
        blocks = []
        for yy in range(8):
            second = zz + core * (yy - zz)
            blocks.append(qw[second, yy + core * (zz - yy)])
        raw += dot(tokens[:, zz * 256 : zz * 256 + 256], jnp.concatenate(blocks, axis=0))
    for head in range(4):
        cols = slice(head * HEAD, head * HEAD + HEAD)
        queries_ref[:, cols] = normalize(raw[:, cols], q_gain[...]).astype(BF)
    kv_raw = raw[:, 512:QKV]
    kv_ref[...] = jnp.where(t < KV_HEADS, normalize(kv_raw, k_gain[...]), kv_raw).astype(BF)

    @pl.loop(1, 8)
    def _(i):
        d = (t + i) % 8
        left(partial.at[d], rs_send.at[d], rs_recv.at[d])
        left(normed_out.at[0], nb_send.at[d], nb_recv.at[d])
        left(sums_out.at[d], sums_send.at[d], sums_recv.at[d])
        left(nx.at[t], nx_send.at[d], nx_recv.at[d])
        n = (a + i) % 8
        left(qw.at[b, a], q1_send.at[n], q1_recv.at[n])

    left(wg, pair_send.at[0], pair_recv.at[0])
    left(wu, pair_send.at[1], pair_recv.at[1])
    left(wd.at[0], wd_send.at[0], wd_recv.at[0])
    left(wd.at[0], wd_send.at[1], wd_recv.at[1])
    left(wd.at[0], wd_send.at[2], wd_recv.at[2])
    for step in range(4):
        for c in ring(step):
            c.wait_send()
    left(tx.at[0:7], d1_send, d1_recv)
    left(act, act_send, act_recv)
    left(r4.at[0:7], r4_send, r4_recv)
    left(x0, c_send, c_recv0.at[0])
    left(x1, c_send, c_recv0.at[0])

    @pl.when(core == 0)
    def _():
        left(r1.at[0:7], d2_send, d2_recv0.at[0])

        @pl.when(half == 1)
        def _():
            left(r1.at[0], d2_send, d2_recv0.at[0])

    @pl.when(core == 1)
    def _():
        left(r1.at[0:7], d2_send, d2_recv0.at[0])
        left(r1.at[0, 0:4], d2_send, d2_recv0.at[0])

    left(y1.at[0:7], r3_send, r3_recv)

    @pl.when((core == 0) & (half == 0))
    def _():
        left(y0.at[0:3], r3_send, r3_recv)
        left(y1.at[0], r3_send, r3_recv)

    @pl.when((core == 0) & (half == 1))
    def _():
        left(y0, r3_send, r3_recv)
        left(y1.at[0], r3_send, r3_recv)

    @pl.when(core == 1)
    def _():
        left(y0, r3_send, r3_recv)


def per_device(
    attn_out,
    out_weight,
    residual,
    attn_gain,
    expert_ids,
    route_weights,
    w_gate,
    w_up,
    w_down,
    input_gain,
    q_weight,
    kv_weight,
    q_gain,
    k_gain,
):
    any_spec = pl.BlockSpec(memory_space=pl.ANY)
    vmem = pl.BlockSpec(memory_space=pltpu.VMEM)
    dma = pltpu.SemaphoreType.DMA
    rows = (3, 4, QUARTER)

    def buf(*shape):
        return pltpu.VMEM(shape, BF)

    return pl.pallas_call(
        kernel,
        out_shape=(
            jax.ShapeDtypeStruct((TOKENS, D), BF),
            jax.ShapeDtypeStruct((GROUP, 512), BF),
            jax.ShapeDtypeStruct((GROUP, HEAD), BF),
        ),
        in_specs=[
            any_spec,
            any_spec,
            vmem,
            vmem,
            vmem,
            vmem,
            any_spec,
            any_spec,
            any_spec,
            vmem,
            any_spec,
            any_spec,
            vmem,
            vmem,
        ],
        out_specs=(vmem, vmem, vmem),
        scratch_shapes=[
            buf(GROUP, 512),
            buf(512, D),
            buf(D, HIDDEN),
            buf(D, HIDDEN),
            buf(D, HIDDEN),
            buf(D, HIDDEN),
            buf(D, 2 * PAIR_HIDDEN),
            buf(HIDDEN, D),
            buf(4, HIDDEN, D // 2),
            buf(8, 8, 32, QKV),
            buf(8, TOKENS, D),
            buf(8, TOKENS, D),
            buf(4, TOKENS, QUARTER),
            buf(8, TOKENS, QUARTER),
            buf(SLOTS, GROUP),
            buf(GROUP, SLOTS),
            buf(GROUP, SLOTS),
            buf(8, 8, *rows),
            buf(8, 8, *rows),
            buf(4, 8, *rows),
            buf(8, 4, *rows),
            buf(4, 8, *rows),
            buf(8, 4, *rows),
            pltpu.VMEM((ROWS, 2 * PAIR_HIDDEN), F32),
            buf(ROWS, PAIR_HIDDEN),
            buf(ROWS, PAIR_HIDDEN),
            pltpu.VMEM((ROWS, D // 2), F32),
            buf(4, 8, *rows),
            buf(8, 4, *rows),
            buf(8, 8, *rows),
            buf(8, 8, *rows),
            buf(8, TOKENS, QUARTER),
            buf(8, TOKENS, QUARTER),
            buf(TOKENS, D),
            buf(8, TOKENS, D),
            dma((7,)),
            dma((8,)),
            dma((8,)),
            dma((8,)),
            dma((8,)),
            dma((2,)),
            dma((2,)),
            dma((3,)),
            dma((3,)),
            dma((8,)),
            dma((8,)),
            dma((4, 2)),
            dma((4, 2)),
            dma,
            dma,
            dma,
            dma((4,)),
            dma((8,)),
            dma,
            dma((4,)),
            dma((8,)),
            dma,
            dma,
            dma,
            dma,
            dma,
            dma,
            dma((8,)),
            dma((8,)),
            dma((8,)),
            dma((8,)),
        ],
        compiler_params=pltpu.CompilerParams(
            collective_id=0, has_side_effects=True, vmem_limit_bytes=56 * 1024 * 1024
        ),
    )(
        attn_out,
        out_weight,
        residual,
        attn_gain.reshape(1, -1),
        expert_ids,
        route_weights,
        w_gate,
        w_up,
        w_down,
        input_gain.reshape(1, -1),
        q_weight,
        kv_weight,
        q_gain.reshape(1, -1),
        k_gain.reshape(1, -1),
    )


def solution(mesh):
    return jax.shard_map(
        per_device,
        mesh=mesh,
        in_specs=(
            P("expert", "tensor"),
            P("tensor", None),
            P(("expert", "tensor"), None),
            P(),
            P("expert", None),
            P("expert", None),
            P("expert", None, "tensor"),
            P("expert", None, "tensor"),
            P("expert", "tensor", None),
            P(),
            P("expert", "tensor"),
            P("expert", "tensor"),
            P(),
            P(),
        ),
        out_specs=(P(("expert", "tensor"), None), P("expert", "tensor"), P("expert", "tensor")),
        check_vma=False,
    )
```

```python
import jax
import jax.numpy as jnp
from jax import lax
from jax.experimental import pallas as pl
from jax.experimental.pallas import tpu as pltpu
from jax.sharding import PartitionSpec as P

MESH = pl.DeviceIdType.MESH
BF = jnp.bfloat16
F32 = jnp.float32

KV_HEADS = 4
TOP = 8
EPSILON = 1e-06

D = 2048
GROUP = 128
TOKENS = 16
CAP = 12
QUARTER = 512
PIECE = 256
FIRST = 4
HIDDEN = 192
PAIR_HIDDEN = 384
ROWS = 384
SLOTS = 768
QKV = 640
HEAD = 128


def normalize(values, gain):
    return values * lax.rsqrt(jnp.mean(values * values, axis=-1, keepdims=True) + EPSILON) * gain


def dot(a, b):
    return jnp.dot(a, b, preferred_element_type=F32)


def iota(shape, axis):
    return lax.broadcasted_iota(jnp.int32, shape, axis)


def kernel(
    attn_hbm,
    ow_hbm,
    res_ref,
    attn_gain,
    ids_ref,
    rw_ref,
    wg_hbm,
    wu_hbm,
    wd_hbm,
    input_gain,
    qw_hbm,
    kvw_hbm,
    moved_ref,
    raw_ref,
    attn,
    ow,
    gate_up,
    wd_own,
    wd,
    qw,
    partial,
    rs_in,
    normed_out,
    normed_in,
    pick,
    mix_hi,
    mix_lo,
    tx,
    r1,
    x0,
    x1,
    c0,
    c1,
    hidden,
    act,
    act_in,
    y_acc,
    y0,
    y1,
    r3,
    r4,
    sums_out,
    sums_in,
    first,
    nx,
    load_sem,
    rs_send,
    rs_recv,
    nb_send,
    nb_recv,
    pair_send,
    pair_recv,
    wd_send,
    wd_recv,
    q1_send,
    q1_recv,
    q2_send,
    q2_recv,
    d1_send,
    d1_recv,
    d2_send,
    d2_recv0,
    d2_recv1,
    c_send,
    c_recv0,
    c_recv1,
    act_send,
    act_recv,
    r3_send,
    r3_recv,
    r4_send,
    r4_recv,
    sums_send,
    sums_recv,
    nx_send,
    nx_recv,
):
    e = lax.axis_index("expert")
    t = lax.axis_index("tensor")
    z, y = e // 8, e % 8
    core = t % 2
    side = (t // 2) % 2
    parity = t // 4
    partner = t + 1 - 2 * core
    cross = t + 2 - 4 * side
    core0, core1 = t - core, t - core + 1
    half = z // 4
    a = y + core * (z - y)
    b = z + core * (y - z)

    def at(first_axis, second_axis):
        return (second_axis + core * (first_axis - second_axis)) * 8 + (
            first_axis + core * (second_axis - first_axis)
        )

    def step_of(i):
        return jnp.where(i % 2 == 1, (i + 1) // 2, 8 - i // 2)

    def remote(src, dst, send, recv, expert, tensor):
        return pltpu.make_async_remote_copy(
            src_ref=src,
            dst_ref=dst,
            send_sem=send,
            recv_sem=recv,
            device_id={"expert": expert, "tensor": tensor},
            device_id_type=MESH,
        )

    def arrived(dst, send, recv):
        remote(dst, dst, send, recv, e, partner).wait_recv()

    def left(src, send, recv):
        remote(src, src, send, recv, e, partner).wait_send()

    sent, coming = [], {}

    def send(src, dst, send_sem, recv_sem, expert, tensor):
        remote(src, dst, send_sem, recv_sem, expert, tensor).start()
        sent.append(lambda: left(src, send_sem, recv_sem))

    def expect(name, dst, send_sem, recv_sem):
        coming.setdefault(name, []).append(lambda: arrived(dst, send_sem, recv_sem))

    def take(name):
        for wait in coming.pop(name):
            wait()

    def to_tensor(name, src_of, dst, send_sem, recv_sem):
        @pl.loop(1, 8)
        def _(i):
            d = (t + i) % 8
            remote(src_of(d), dst.at[t], send_sem.at[d], recv_sem.at[t], e, d).start()

        def waits():
            @pl.loop(1, 8)
            def _(i):
                s = (t + i) % 8
                arrived(dst.at[s], send_sem.at[s], recv_sem.at[s])

        def gone():
            @pl.loop(1, 8)
            def _(i):
                d = (t + i) % 8
                left(src_of(d), send_sem.at[d], recv_sem.at[d])

        coming[name] = [waits]
        sent.append(gone)

    barrier = pltpu.get_barrier_semaphore()

    @pl.loop(1, 8)
    def _(i):
        pl.semaphore_signal(
            barrier, inc=1, device_id={"expert": e, "tensor": (t + i) % 8}, device_id_type=MESH
        )
        for which in (core0, core1):
            pl.semaphore_signal(
                barrier,
                inc=1,
                device_id={"expert": z * 8 + (y + i) % 8, "tensor": which},
                device_id_type=MESH,
            )
            pl.semaphore_signal(
                barrier,
                inc=1,
                device_id={"expert": ((z + i) % 8) * 8 + y, "tensor": which},
                device_id_type=MESH,
            )

    ow_parts = [
        pltpu.make_async_copy(
            ow_hbm.at[:, pl.ds(n * 512, 512)], ow.at[:, pl.ds(n * 512, 512)], load_sem.at[6 + n]
        )
        for n in range(4)
    ]
    loads = [
        pltpu.make_async_copy(attn_hbm, attn, load_sem.at[0]),
        pltpu.make_async_copy(qw_hbm, qw.at[b, a, :, pl.ds(0, 512)], load_sem.at[1]),
        pltpu.make_async_copy(kvw_hbm, qw.at[b, a, :, pl.ds(512, 128)], load_sem.at[2]),
        pltpu.make_async_copy(wg_hbm.at[0], gate_up.at[0], load_sem.at[3]),
        pltpu.make_async_copy(wu_hbm.at[0], gate_up.at[2], load_sem.at[4]),
        pltpu.make_async_copy(wd_hbm.at[0], wd_own, load_sem.at[5]),
    ]
    loads[0].start()
    for part in ow_parts:
        part.start()
    for load in loads[1:]:
        load.start()

    loads[0].wait()
    for n in range(4):
        ow_parts[n].wait()
        cols = slice(n * 512, n * 512 + 512)
        partial[:, :, cols] = dot(attn[...], ow[:, cols]).astype(BF).reshape(8, TOKENS, 512)

    pl.semaphore_wait(barrier, 35)

    to_tensor("rs", lambda d: partial.at[d], rs_in, rs_send, rs_recv)

    loads[1].wait()
    loads[2].wait()

    @pl.loop(1, 8)
    def _(i):
        d = (a + step_of(i)) % 8
        remote(
            qw.at[b, a], qw.at[b, a], q1_send.at[d], q1_recv.at[a], at(d, b), t
        ).start()

    def q1_left():
        @pl.loop(1, 8)
        def _(i):
            n = (a + i) % 8
            left(qw.at[b, a], q1_send.at[n], q1_recv.at[n])

    sent.append(q1_left)

    loads[3].wait()
    loads[4].wait()
    for k in range(2):
        send(gate_up.at[2 * k], gate_up.at[2 * k + 1], pair_send.at[k], pair_recv.at[k], e, partner)
        expect("pair", gate_up.at[2 * k + 1], pair_send.at[k], pair_recv.at[k])

    position = iota((GROUP, 64), 1)
    p_first, p_second = position // 8, position % 8
    expert_of = 2 * at(p_first, p_second) + parity
    ids = ids_ref[...].T
    weights = rw_ref[...].T
    named = jnp.zeros((GROUP, 64), F32)
    weight_of = jnp.zeros((GROUP, 64), F32)
    for k in range(TOP):
        hit = expert_of == ids[:, k : k + 1]
        named += jnp.where(hit, 1.0, 0.0)
        weight_of += jnp.where(hit, weights[:, k : k + 1], 0.0)
    lower = jnp.where(iota((GROUP, GROUP), 1) < iota((GROUP, GROUP), 0), 1.0, 0.0).astype(BF)
    rank = dot(lower, named.astype(BF))
    code = (named * (rank + 1.0)).astype(BF)
    slot = iota((64, SLOTS), 1)
    start = iota((64, SLOTS), 0) * CAP
    spread = jnp.where((slot >= start) & (slot < start + CAP), 1.0, 0.0).astype(BF)
    wanted = (iota((GROUP, SLOTS), 1) % CAP + 1).astype(F32)
    chosen = dot(code, spread) == wanted
    high = weight_of.astype(BF)
    low = (weight_of - high.astype(F32)).astype(BF)
    mix_hi[...] = jnp.where(chosen, dot(high, spread), 0.0).astype(BF)
    mix_lo[...] = jnp.where(chosen, dot(low, spread), 0.0).astype(BF)
    pick[...] = jnp.where(chosen, 1.0, 0.0).T.astype(BF)

    after, before = at(a, (b + 1) % 8), at(a, (b + 7) % 8)

    def ring(step):
        rows = ((b + 8 - step) % 8, (b + step) % 8)
        if step == 3:
            pieces = (qw.at[rows[0], pl.ds(0, 4)], qw.at[rows[1], pl.ds(4, 4)])
        else:
            pieces = (qw.at[rows[0]], qw.at[rows[1]])
        return [
            remote(pieces[k], pieces[k], q2_send.at[step, k], q2_recv.at[step, k], (after, before)[k], t)
            for k in range(2)
        ]

    def ring_wait(step):
        rows = ((b + 7 - step) % 8, (b + 1 + step) % 8)
        if step == 3:
            pieces = (qw.at[rows[0], pl.ds(0, 4)], qw.at[rows[1], pl.ds(4, 4)])
        else:
            pieces = (qw.at[rows[0]], qw.at[rows[1]])
        for k in range(2):
            arrived(pieces[k], q2_send.at[step, k], q2_recv.at[step, k])

    @pl.loop(1, 8)
    def _(i):
        s = (a + i) % 8
        arrived(qw.at[b, s], q1_send.at[s], q1_recv.at[s])

    def ring_start(step):
        for c in ring(step):
            c.start()
        sent.append(lambda: [c.wait_send() for c in ring(step)])
        coming["ring"] = [lambda: ring_wait(step)]

    ring_start(0)

    rs_in[t] = partial[t]

    take("rs")

    total = res_ref[...].astype(F32)
    attn_sum = rs_in[0].astype(F32)
    for k in range(1, 8):
        attn_sum += rs_in[k].astype(F32)
    first_residual = (total + attn_sum).astype(BF)
    first[...] = first_residual
    normed = normalize(first_residual.astype(F32), attn_gain[...]).astype(BF)
    for s in range(4):
        normed_out[s] = normed[:, s * QUARTER : s * QUARTER + QUARTER]
    normed_in[t] = normed_out[t % 4]

    to_tensor("nb", lambda d: normed_out.at[d % 4], normed_in, nb_send, nb_recv)

    loads[5].wait()
    own_half = pl.ds(pl.multiple_of(side * 1024, 1024), 1024)
    other_half = pl.ds(pl.multiple_of((1 - side) * 1024, 1024), 1024)
    send(wd_own.at[:, own_half], wd.at[1], wd_send.at[0], wd_recv.at[0], e, partner)
    expect("wd", wd.at[1], wd_send.at[0], wd_recv.at[0])
    send(wd_own.at[:, other_half], wd.at[2], wd_send.at[1], wd_recv.at[1], e, cross)
    expect("wd cross", wd.at[2], wd_send.at[1], wd_recv.at[1])
    wd[0] = wd_own[:, own_half]

    take("nb")

    group = normed_in[...].reshape(GROUP, QUARTER)

    def gone_d2():
        @pl.when(core == 0)
        def _():
            left(r1.at[0, pl.ds(0, 7)], d2_send, d2_recv0.at[0, 0])

            @pl.when(half == 1)
            def _():
                left(r1.at[0, 0], d2_send, d2_recv0.at[0, 0])

        @pl.when(core == 1)
        def _():
            left(r1.at[0, pl.ds(0, 7)], d2_send, d2_recv0.at[0, 0])
            left(r1.at[0, 0, pl.ds(0, 4)], d2_send, d2_recv0.at[0, 0])

    def dispatch_first(p):
        for k in range(2):
            rows = slice(k * 384, k * 384 + 384)
            tx[p, 4 * k : 4 * k + 4] = (
                dot(pick[rows, :], group[:, p * PIECE : p * PIECE + PIECE])
                .astype(BF)
                .reshape(4, 8, 3, 4, PIECE)
            )

        @pl.loop(1, 8)
        def _(i):
            d = (a + step_of(i)) % 8
            remote(tx.at[p, d], r1.at[p, a], d1_send, d1_recv.at[p], at(d, b), t).start()

        pltpu.make_async_copy(tx.at[p, a], r1.at[p, a], d1_recv.at[p]).start()
        sent.append(lambda: left(tx.at[p, pl.ds(0, 7)], d1_send, d1_recv.at[p]))

    def dispatch_second(p):
        arrived(r1.at[p], d1_send, d1_recv.at[p])

        def core0_path(d):
            return r1.at[p, :, d], x0.at[p, z % 4], d2_recv0.at[p, z % 4]

        def core1_path(d, hf):
            return r1.at[p, pl.ds(4 * hf, 4), d], x1.at[p, y], d2_recv1.at[p, y]

        @pl.when(core == 0)
        def _():
            src, dst, sem = core0_path(b)

            @pl.when(half == 0)
            def _():
                pltpu.make_async_copy(src, dst, sem).start()

            @pl.when(half == 1)
            def _():
                remote(src, dst, d2_send, sem, e, core1).start()

            @pl.loop(1, 8)
            def _(i):
                d = (b + step_of(i)) % 8
                src, dst, sem = core0_path(d)
                remote(src, dst, d2_send, sem, at(a, d), core0 + half).start()

        @pl.when(core == 1)
        def _():
            src, dst, sem = core1_path(b, 0)
            remote(src, dst, d2_send, sem, e, core0).start()
            src, dst, sem = core1_path(b, 1)
            pltpu.make_async_copy(src, dst, sem).start()

            @pl.loop(1, 8)
            def _(i):
                d = (b + step_of(i)) % 8
                for hf in range(2):
                    src, dst, sem = core1_path(d, hf)
                    remote(src, dst, d2_send, sem, at(a, d), core0 + hf).start()

        sent.append(gone_d2)

    def forward0(p, k):
        arrived(x0.at[p, k], c_send, d2_recv0.at[p, k])
        remote(x0.at[p, k], c0.at[p, k], c_send, c_recv0.at[p, k], e, cross).start()

    def forward1(p, i):
        k = (y + step_of(i)) % 8
        arrived(x1.at[p, k], c_send, d2_recv1.at[p, k])
        remote(x1.at[p, k], c1.at[p, k], c_send, c_recv1.at[p, k], e, cross).start()

    def forward_rest(p):
        @pl.loop(0, 4)
        def _(i):
            forward0(p, i)

            @pl.when(i >= FIRST // 2)
            def _():
                forward1(p, 2 * i)
                forward1(p, 2 * i + 1)

        sent.append(lambda: (left(x0.at[p], c_send, c_recv0.at[p, 0]), left(x1.at[p], c_send, c_recv0.at[p, 0])))

    def forward_first(p):
        @pl.loop(0, FIRST)
        def _(i):
            forward1(p, i)

    def take_c0(p):
        @pl.loop(0, 4)
        def _(i):
            arrived(c0.at[p, i], c_send, c_recv0.at[p, i])

    def take_c1(p):
        @pl.loop(0, 8)
        def _(i):
            arrived(c1.at[p, i], c_send, c_recv1.at[p, i])

    def multiply(values, column, zero=False):
        rows = pl.ds(pl.multiple_of(column, PIECE), PIECE)
        for n in range(2):
            cols = slice(n * PAIR_HIDDEN, n * PAIR_HIDDEN + PAIR_HIDDEN)
            product = lax.dot_general(
                values,
                gate_up[2 * n : 2 * n + 2, :, rows].reshape(PAIR_HIDDEN, PIECE),
                (((1,), (1,)), ((), ())),
                preferred_element_type=F32,
            )
            hidden[:, cols] = product if zero else hidden[:, cols] + product

    def natural(ref, p):
        return ref[p].reshape(ROWS, PIECE)

    def turned(ref, p):
        return jnp.concatenate([ref[p, :, k].reshape(96, PIECE) for k in range(4)], axis=0)

    own, other = side * 1024, (1 - side) * 1024

    dispatch_first(0)
    dispatch_first(1)
    take("pair")
    take("wd cross")
    send(wd.at[2], wd.at[3], wd_send.at[2], wd_recv.at[2], e, partner)
    expect("wd", wd.at[3], wd_send.at[2], wd_recv.at[2])
    dispatch_second(0)
    forward_first(0)
    dispatch_second(1)
    forward_rest(0)
    multiply(natural(x0, 0), own, True)
    multiply(turned(x1, 0), own + QUARTER)
    forward_first(1)
    forward_rest(1)
    take("ring")
    ring_start(1)
    multiply(natural(x0, 1), own + PIECE)
    multiply(turned(x1, 1), own + QUARTER + PIECE)
    take_c0(0)
    multiply(natural(c0, 0), other)
    take_c1(0)
    multiply(turned(c1, 0), other + QUARTER)
    take("ring")
    ring_start(2)
    take_c0(1)
    multiply(natural(c0, 1), other + PIECE)
    take_c1(1)
    multiply(turned(c1, 1), other + QUARTER + PIECE)

    gate = hidden[:, 0:PAIR_HIDDEN]
    act[...] = (
        gate * (1.0 / (1.0 + jnp.exp(-gate))) * hidden[:, PAIR_HIDDEN : 2 * PAIR_HIDDEN]
    ).astype(BF)
    send(act, act_in, act_send, act_recv, e, cross)

    take("wd")
    for n in range(4):
        cols = slice(n * 256, n * 256 + 256)
        y_acc[:, cols] = dot(act[...], wd[0:2, :, cols].reshape(PAIR_HIDDEN, 256))
    take("ring")
    ring_start(3)
    arrived(act_in, act_send, act_recv)

    first_zone = 4 * core

    def gone_r3():
        left(y1.at[0, pl.ds(0, 7)], r3_send, r3_recv.at[0])

        @pl.when((core == 0) & (half == 0))
        def _():
            left(y0.at[0, pl.ds(0, 3)], r3_send, r3_recv.at[0])
            left(y1.at[0, 0], r3_send, r3_recv.at[0])

        @pl.when((core == 0) & (half == 1))
        def _():
            left(y0.at[0], r3_send, r3_recv.at[0])
            left(y1.at[0, 0], r3_send, r3_recv.at[0])

        @pl.when(core == 1)
        def _():
            left(y0.at[0], r3_send, r3_recv.at[0])

    for p in range(2):
        for n in (p, 2 + p):
            cols = slice(n * PIECE, n * PIECE + PIECE)
            out = y_acc[:, cols] + dot(act_in[...], wd[2:4, :, cols].reshape(PAIR_HIDDEN, PIECE))
            blocks = out.astype(BF).reshape(4, 8, 3, 4, PIECE)
            if n < 2:
                y0[p] = blocks
            else:
                for k in range(4):
                    y1[p, :, k] = blocks[k]

        @pl.loop(0, 4)
        def _(i):
            zone = first_zone + i
            src, dst = y0.at[p, i], r3.at[p, z]

            @pl.when(zone != z)
            def _():
                remote(src, dst, r3_send, r3_recv.at[p], zone * 8 + y, core0).start()

            @pl.when((zone == z) & (core == 0))
            def _():
                pltpu.make_async_copy(src, dst, r3_recv.at[p]).start()

            @pl.when((zone == z) & (core == 1))
            def _():
                remote(src, dst, r3_send, r3_recv.at[p], e, core0).start()

        into = r3.at[p, y, pl.ds(first_zone, 4)]

        @pl.loop(1, 8)
        def _(i):
            d = (y + step_of(i)) % 8
            remote(y1.at[p, d], into, r3_send, r3_recv.at[p], z * 8 + d, core1).start()

        @pl.when(core == 1)
        def _():
            pltpu.make_async_copy(y1.at[p, y], into, r3_recv.at[p]).start()

        @pl.when(core == 0)
        def _():
            remote(y1.at[p, y], into, r3_send, r3_recv.at[p], e, core1).start()

        sent.append(gone_r3)

    for p in range(2):
        arrived(r3.at[p], r3_send, r3_recv.at[p])

        @pl.loop(1, 8)
        def _(i):
            d = (a + step_of(i)) % 8
            remote(r3.at[p, :, d], r4.at[p, a], r4_send, r4_recv.at[p], at(d, b), t).start()

        pltpu.make_async_copy(r3.at[p, :, a], r4.at[p, a], r4_recv.at[p]).start()
        sent.append(lambda: left(r4.at[0, pl.ds(0, 7)], r4_send, r4_recv.at[0]))

    for p in range(2):
        arrived(r4.at[p], r4_send, r4_recv.at[p])
        returned = r4[p].reshape(SLOTS, PIECE)
        weighted = dot(mix_hi[...], returned) + dot(mix_lo[...], returned)
        sums_out[:, :, p * PIECE : p * PIECE + PIECE] = weighted.astype(BF).reshape(
            8, TOKENS, PIECE
        )
    sums_in[t] = sums_out[t]

    to_tensor("sums", lambda d: sums_out.at[d], sums_in, sums_send, sums_recv)
    take("sums")

    expert_sum = jnp.concatenate(
        [sums_in[s].astype(F32) + sums_in[s + 4].astype(F32) for s in range(4)], axis=1
    )
    next_residual = (first[...].astype(F32) + expert_sum).astype(BF)
    moved_ref[...] = next_residual
    nx[t] = normalize(next_residual.astype(F32), input_gain[...]).astype(BF)

    to_tensor("nx", lambda d: nx.at[t], nx, nx_send, nx_recv)

    take("ring")

    take("nx")

    tokens = nx[...].reshape(GROUP, D)
    raw = jnp.zeros((GROUP, QKV), F32)
    for zz in range(8):
        blocks = []
        for yy in range(8):
            second = zz + core * (yy - zz)
            blocks.append(qw[second, yy + core * (zz - yy)])
        raw += dot(tokens[:, zz * 256 : zz * 256 + 256], jnp.concatenate(blocks, axis=0))
    raw_ref[...] = raw

    for gone in sent:
        gone()


def finish(moved_ref, raw_ref, q_gain, k_gain, next_ref, queries_ref, kv_ref):
    t = lax.axis_index("tensor")
    next_ref[...] = moved_ref[...]
    for head in range(4):
        cols = slice(head * HEAD, head * HEAD + HEAD)
        queries_ref[:, cols] = normalize(raw_ref[:, cols], q_gain[...]).astype(BF)
    kv_raw = raw_ref[:, 512:QKV]
    kv_ref[...] = jnp.where(t < KV_HEADS, normalize(kv_raw, k_gain[...]), kv_raw).astype(BF)


def per_device(
    attn_out,
    out_weight,
    residual,
    attn_gain,
    expert_ids,
    route_weights,
    w_gate,
    w_up,
    w_down,
    input_gain,
    q_weight,
    kv_weight,
    q_gain,
    k_gain,
):
    any_spec = pl.BlockSpec(memory_space=pl.ANY)
    vmem = pl.BlockSpec(memory_space=pltpu.VMEM)
    dma = pltpu.SemaphoreType.DMA
    rows = (3, 4, PIECE)

    def buf(*shape):
        return pltpu.VMEM(shape, BF)

    moved, raw = pl.pallas_call(
        kernel,
        out_shape=(
            jax.ShapeDtypeStruct((TOKENS, D), BF),
            jax.ShapeDtypeStruct((GROUP, QKV), F32),
        ),
        in_specs=[
            any_spec,
            any_spec,
            vmem,
            vmem,
            vmem,
            vmem,
            any_spec,
            any_spec,
            any_spec,
            vmem,
            any_spec,
            any_spec,
        ],
        out_specs=(vmem, vmem),
        scratch_shapes=[
            buf(GROUP, 512),
            buf(512, D),
            buf(4, HIDDEN, D),
            buf(HIDDEN, D),
            buf(4, HIDDEN, D // 2),
            buf(8, 8, 32, QKV),
            buf(8, TOKENS, D),
            buf(8, TOKENS, D),
            buf(4, TOKENS, QUARTER),
            buf(8, TOKENS, QUARTER),
            buf(SLOTS, GROUP),
            buf(GROUP, SLOTS),
            buf(GROUP, SLOTS),
            buf(2, 8, 8, *rows),
            buf(2, 8, 8, *rows),
            buf(2, 4, 8, *rows),
            buf(2, 8, 4, *rows),
            buf(2, 4, 8, *rows),
            buf(2, 8, 4, *rows),
            pltpu.VMEM((ROWS, 2 * PAIR_HIDDEN), F32),
            buf(ROWS, PAIR_HIDDEN),
            buf(ROWS, PAIR_HIDDEN),
            pltpu.VMEM((ROWS, D // 2), F32),
            buf(2, 4, 8, *rows),
            buf(2, 8, 4, *rows),
            buf(2, 8, 8, *rows),
            buf(2, 8, 8, *rows),
            buf(8, TOKENS, QUARTER),
            buf(8, TOKENS, QUARTER),
            buf(TOKENS, D),
            buf(8, TOKENS, D),
            dma((10,)),
            dma((8,)),
            dma((8,)),
            dma((8,)),
            dma((8,)),
            dma((2,)),
            dma((2,)),
            dma((3,)),
            dma((3,)),
            dma((8,)),
            dma((8,)),
            dma((4, 2)),
            dma((4, 2)),
            dma,
            dma((2,)),
            dma,
            dma((2, 4)),
            dma((2, 8)),
            dma,
            dma((2, 4)),
            dma((2, 8)),
            dma,
            dma,
            dma,
            dma((2,)),
            dma,
            dma((2,)),
            dma((8,)),
            dma((8,)),
            dma((8,)),
            dma((8,)),
        ],
        compiler_params=pltpu.CompilerParams(
            collective_id=0, has_side_effects=True, vmem_limit_bytes=66_400_000
        ),
    )(
        attn_out,
        out_weight,
        residual,
        attn_gain.reshape(1, -1),
        expert_ids.T,
        route_weights.T,
        jnp.swapaxes(w_gate, 1, 2),
        jnp.swapaxes(w_up, 1, 2),
        w_down,
        input_gain.reshape(1, -1),
        q_weight,
        kv_weight,
    )
    return pl.pallas_call(
        finish,
        out_shape=(
            jax.ShapeDtypeStruct((TOKENS, D), BF),
            jax.ShapeDtypeStruct((GROUP, 512), BF),
            jax.ShapeDtypeStruct((GROUP, HEAD), BF),
        ),
        in_specs=[vmem] * 4,
        out_specs=(vmem, vmem, vmem),
        compiler_params=pltpu.CompilerParams(vmem_limit_bytes=4 * 1024 * 1024),
    )(moved, raw, q_gain.reshape(1, -1), k_gain.reshape(1, -1))


def solution(mesh):
    return jax.shard_map(
        per_device,
        mesh=mesh,
        in_specs=(
            P("expert", "tensor"),
            P("tensor", None),
            P(("expert", "tensor"), None),
            P(),
            P("expert", None),
            P("expert", None),
            P("expert", None, "tensor"),
            P("expert", None, "tensor"),
            P("expert", "tensor", None),
            P(),
            P("expert", "tensor"),
            P("expert", "tensor"),
            P(),
            P(),
        ),
        out_specs=(P(("expert", "tensor"), None), P("expert", "tensor"), P("expert", "tensor")),
        check_vma=False,
    )
```

```python
import jax
import jax.numpy as jnp
from jax import lax
from jax.experimental import pallas as pl
from jax.experimental.pallas import tpu as pltpu
from jax.sharding import PartitionSpec as P

MESH = pl.DeviceIdType.MESH
BF = jnp.bfloat16
F32 = jnp.float32

KV_HEADS = 4
TOP = 8
EPSILON = 1e-06

D = 2048
GROUP = 128
TOKENS = 16
CAP = 12
QUARTER = 512
PIECE = 256
FIRST = 4
HIDDEN = 192
PAIR_HIDDEN = 384
ROWS = 384
SLOTS = 768
QKV = 640
HEAD = 128


def normalize(values, gain):
    return values * lax.rsqrt(jnp.mean(values * values, axis=-1, keepdims=True) + EPSILON) * gain


def dot(a, b):
    return jnp.dot(a, b, preferred_element_type=F32)


def iota(shape, axis):
    return lax.broadcasted_iota(jnp.int32, shape, axis)


def kernel(
    attn_hbm,
    ow_hbm,
    res_ref,
    attn_gain,
    ids_ref,
    rw_ref,
    wg_hbm,
    wu_hbm,
    wd_hbm,
    input_gain,
    qw_hbm,
    kvw_hbm,
    moved_ref,
    raw_ref,
    attn,
    ow,
    gate_up,
    wd_own,
    wd,
    qw,
    partial,
    mates,
    sums_of_chip,
    rs_in,
    normed_out,
    normed_in,
    pick,
    mix_hi,
    mix_lo,
    tx,
    r1,
    x0,
    x1,
    c0,
    c1,
    hidden,
    act,
    act_in,
    y_acc,
    y0,
    y1,
    r3,
    r4,
    sums_out,
    sums_in,
    first,
    nx,
    load_sem,
    mate_send,
    mate_recv,
    rs_send,
    rs_recv,
    nb_send,
    nb_recv,
    pair_send,
    pair_recv,
    wd_send,
    wd_recv,
    q1_send,
    q1_recv,
    q2_send,
    q2_recv,
    d1_send,
    d1_recv,
    d2_send,
    d2_recv0,
    d2_recv1,
    c_send,
    c_recv0,
    c_recv1,
    act_send,
    act_recv,
    r3_send,
    r3_recv,
    r4_send,
    r4_recv,
    sums_send,
    sums_recv,
    nx_send,
    nx_recv,
):
    e = lax.axis_index("expert")
    t = lax.axis_index("tensor")
    z, y = e // 8, e % 8
    core = t % 2
    side = (t // 2) % 2
    parity = t // 4
    chip = t // 2
    partner = t + 1 - 2 * core
    cross = t + 2 - 4 * side
    core0, core1 = t - core, t - core + 1
    half = z // 4
    a = y + core * (z - y)
    b = z + core * (y - z)

    def at(first_axis, second_axis):
        return (second_axis + core * (first_axis - second_axis)) * 8 + (
            first_axis + core * (second_axis - first_axis)
        )

    def step_of(i):
        return jnp.where(i % 2 == 1, (i + 1) // 2, 8 - i // 2)

    def remote(src, dst, send, recv, expert, tensor):
        return pltpu.make_async_remote_copy(
            src_ref=src,
            dst_ref=dst,
            send_sem=send,
            recv_sem=recv,
            device_id={"expert": expert, "tensor": tensor},
            device_id_type=MESH,
        )

    def arrived(dst, send, recv):
        remote(dst, dst, send, recv, e, partner).wait_recv()

    def left(src, send, recv):
        remote(src, src, send, recv, e, partner).wait_send()

    sent, coming = [], {}

    def send(src, dst, send_sem, recv_sem, expert, tensor):
        remote(src, dst, send_sem, recv_sem, expert, tensor).start()
        sent.append(lambda: left(src, send_sem, recv_sem))

    def expect(name, dst, send_sem, recv_sem):
        coming.setdefault(name, []).append(lambda: arrived(dst, send_sem, recv_sem))

    def take(name):
        for wait in coming.pop(name):
            wait()

    def to_tensor(name, src_of, dst, send_sem, recv_sem):
        @pl.loop(1, 8)
        def _(i):
            d = (t + i) % 8
            remote(src_of(d), dst.at[t], send_sem.at[d], recv_sem.at[t], e, d).start()

        def waits():
            @pl.loop(1, 8)
            def _(i):
                s = (t + i) % 8
                arrived(dst.at[s], send_sem.at[s], recv_sem.at[s])

        def gone():
            @pl.loop(1, 8)
            def _(i):
                d = (t + i) % 8
                left(src_of(d), send_sem.at[d], recv_sem.at[d])

        coming[name] = [waits]
        sent.append(gone)

    barrier = pltpu.get_barrier_semaphore()

    @pl.loop(1, 8)
    def _(i):
        pl.semaphore_signal(
            barrier, inc=1, device_id={"expert": e, "tensor": (t + i) % 8}, device_id_type=MESH
        )
        for which in (core0, core1):
            pl.semaphore_signal(
                barrier,
                inc=1,
                device_id={"expert": z * 8 + (y + i) % 8, "tensor": which},
                device_id_type=MESH,
            )
            pl.semaphore_signal(
                barrier,
                inc=1,
                device_id={"expert": ((z + i) % 8) * 8 + y, "tensor": which},
                device_id_type=MESH,
            )

    ow_parts = [
        pltpu.make_async_copy(
            ow_hbm.at[:, pl.ds(n * 512, 512)], ow.at[:, pl.ds(n * 512, 512)], load_sem.at[6 + n]
        )
        for n in range(4)
    ]
    loads = [
        pltpu.make_async_copy(attn_hbm, attn, load_sem.at[0]),
        pltpu.make_async_copy(qw_hbm, qw.at[b, a, :, pl.ds(0, 512)], load_sem.at[1]),
        pltpu.make_async_copy(kvw_hbm, qw.at[b, a, :, pl.ds(512, 128)], load_sem.at[2]),
        pltpu.make_async_copy(wg_hbm.at[0], gate_up.at[0], load_sem.at[3]),
        pltpu.make_async_copy(wu_hbm.at[0], gate_up.at[2], load_sem.at[4]),
        pltpu.make_async_copy(wd_hbm.at[0], wd_own, load_sem.at[5]),
    ]
    loads[0].start()
    for part in ow_parts:
        part.start()
    for load in loads[1:]:
        load.start()

    loads[0].wait()
    for n in range(4):
        ow_parts[n].wait()
        cols = slice(n * 512, n * 512 + 512)
        partial[:, :, cols] = dot(attn[...], ow[:, cols]).astype(BF).reshape(8, TOKENS, 512)

    pl.semaphore_wait(barrier, 35)

    for k in range(4):
        theirs = 2 * k + 1 - core
        send(partial.at[theirs], mates.at[k], mate_send.at[k], mate_recv.at[k], e, partner)

    def chip_sum(k):
        arrived(mates.at[k], mate_send.at[k], mate_recv.at[k])
        return (partial[2 * k + core].astype(F32) + mates[k].astype(F32)).astype(BF)

    for i in (2, 1, 3):
        k = (chip + i) % 4
        sums_of_chip[k] = chip_sum(k)
        send(sums_of_chip.at[k], rs_in.at[chip], rs_send.at[k], rs_recv.at[chip], e, 2 * k + core)
        expect("rs", rs_in.at[k], rs_send.at[k], rs_recv.at[k])
    rs_in[chip] = chip_sum(chip)

    loads[1].wait()
    loads[2].wait()

    @pl.loop(1, 8)
    def _(i):
        d = (a + step_of(i)) % 8
        remote(
            qw.at[b, a], qw.at[b, a], q1_send.at[d], q1_recv.at[a], at(d, b), t
        ).start()

    def q1_left():
        @pl.loop(1, 8)
        def _(i):
            n = (a + i) % 8
            left(qw.at[b, a], q1_send.at[n], q1_recv.at[n])

    sent.append(q1_left)

    loads[3].wait()
    loads[4].wait()
    for k in range(2):
        send(gate_up.at[2 * k], gate_up.at[2 * k + 1], pair_send.at[k], pair_recv.at[k], e, partner)
        expect("pair", gate_up.at[2 * k + 1], pair_send.at[k], pair_recv.at[k])

    position = iota((GROUP, 64), 1)
    p_first, p_second = position // 8, position % 8
    expert_of = 2 * at(p_first, p_second) + parity
    ids = ids_ref[...].T
    weights = rw_ref[...].T
    named = jnp.zeros((GROUP, 64), F32)
    weight_of = jnp.zeros((GROUP, 64), F32)
    for k in range(TOP):
        hit = expert_of == ids[:, k : k + 1]
        named += jnp.where(hit, 1.0, 0.0)
        weight_of += jnp.where(hit, weights[:, k : k + 1], 0.0)
    lower = jnp.where(iota((GROUP, GROUP), 1) < iota((GROUP, GROUP), 0), 1.0, 0.0).astype(BF)
    rank = dot(lower, named.astype(BF))
    code = (named * (rank + 1.0)).astype(BF)
    slot = iota((64, SLOTS), 1)
    start = iota((64, SLOTS), 0) * CAP
    spread = jnp.where((slot >= start) & (slot < start + CAP), 1.0, 0.0).astype(BF)
    wanted = (iota((GROUP, SLOTS), 1) % CAP + 1).astype(F32)
    chosen = dot(code, spread) == wanted
    high = weight_of.astype(BF)
    low = (weight_of - high.astype(F32)).astype(BF)
    mix_hi[...] = jnp.where(chosen, dot(high, spread), 0.0).astype(BF)
    mix_lo[...] = jnp.where(chosen, dot(low, spread), 0.0).astype(BF)
    pick[...] = jnp.where(chosen, 1.0, 0.0).T.astype(BF)

    after, before = at(a, (b + 1) % 8), at(a, (b + 7) % 8)

    def ring(step):
        rows = ((b + 8 - step) % 8, (b + step) % 8)
        if step == 3:
            pieces = (qw.at[rows[0], pl.ds(0, 4)], qw.at[rows[1], pl.ds(4, 4)])
        else:
            pieces = (qw.at[rows[0]], qw.at[rows[1]])
        return [
            remote(pieces[k], pieces[k], q2_send.at[step, k], q2_recv.at[step, k], (after, before)[k], t)
            for k in range(2)
        ]

    def ring_wait(step):
        rows = ((b + 7 - step) % 8, (b + 1 + step) % 8)
        if step == 3:
            pieces = (qw.at[rows[0], pl.ds(0, 4)], qw.at[rows[1], pl.ds(4, 4)])
        else:
            pieces = (qw.at[rows[0]], qw.at[rows[1]])
        for k in range(2):
            arrived(pieces[k], q2_send.at[step, k], q2_recv.at[step, k])

    @pl.loop(1, 8)
    def _(i):
        s = (a + i) % 8
        arrived(qw.at[b, s], q1_send.at[s], q1_recv.at[s])

    def ring_start(step):
        for c in ring(step):
            c.start()
        sent.append(lambda: [c.wait_send() for c in ring(step)])
        coming["ring"] = [lambda: ring_wait(step)]

    ring_start(0)

    take("rs")

    total = res_ref[...].astype(F32)
    attn_sum = rs_in[0].astype(F32)
    for k in range(1, 4):
        attn_sum += rs_in[k].astype(F32)
    first_residual = (total + attn_sum).astype(BF)
    first[...] = first_residual
    normed = normalize(first_residual.astype(F32), attn_gain[...]).astype(BF)
    for s in range(4):
        normed_out[s] = normed[:, s * QUARTER : s * QUARTER + QUARTER]
    normed_in[t] = normed_out[t % 4]

    to_tensor("nb", lambda d: normed_out.at[d % 4], normed_in, nb_send, nb_recv)

    loads[5].wait()
    own_half = pl.ds(pl.multiple_of(side * 1024, 1024), 1024)
    other_half = pl.ds(pl.multiple_of((1 - side) * 1024, 1024), 1024)
    send(wd_own.at[:, own_half], wd.at[1], wd_send.at[0], wd_recv.at[0], e, partner)
    expect("wd", wd.at[1], wd_send.at[0], wd_recv.at[0])
    send(wd_own.at[:, other_half], wd.at[2], wd_send.at[1], wd_recv.at[1], e, cross)
    expect("wd cross", wd.at[2], wd_send.at[1], wd_recv.at[1])
    wd[0] = wd_own[:, own_half]

    take("nb")

    group = normed_in[...].reshape(GROUP, QUARTER)

    def gone_d2():
        @pl.when(core == 0)
        def _():
            left(r1.at[0, pl.ds(0, 7)], d2_send, d2_recv0.at[0, 0])

            @pl.when(half == 1)
            def _():
                left(r1.at[0, 0], d2_send, d2_recv0.at[0, 0])

        @pl.when(core == 1)
        def _():
            left(r1.at[0, pl.ds(0, 7)], d2_send, d2_recv0.at[0, 0])
            left(r1.at[0, 0, pl.ds(0, 4)], d2_send, d2_recv0.at[0, 0])

    def dispatch_first(p):
        for k in range(2):
            rows = slice(k * 384, k * 384 + 384)
            tx[p, 4 * k : 4 * k + 4] = (
                dot(pick[rows, :], group[:, p * PIECE : p * PIECE + PIECE])
                .astype(BF)
                .reshape(4, 8, 3, 4, PIECE)
            )

        @pl.loop(1, 8)
        def _(i):
            d = (a + step_of(i)) % 8
            remote(tx.at[p, d], r1.at[p, a], d1_send, d1_recv.at[p], at(d, b), t).start()

        pltpu.make_async_copy(tx.at[p, a], r1.at[p, a], d1_recv.at[p]).start()
        sent.append(lambda: left(tx.at[p, pl.ds(0, 7)], d1_send, d1_recv.at[p]))

    def dispatch_second(p):
        arrived(r1.at[p], d1_send, d1_recv.at[p])

        def core0_path(d):
            return r1.at[p, :, d], x0.at[p, z % 4], d2_recv0.at[p, z % 4]

        def core1_path(d, hf):
            return r1.at[p, pl.ds(4 * hf, 4), d], x1.at[p, y], d2_recv1.at[p, y]

        @pl.when(core == 0)
        def _():
            src, dst, sem = core0_path(b)

            @pl.when(half == 0)
            def _():
                pltpu.make_async_copy(src, dst, sem).start()

            @pl.when(half == 1)
            def _():
                remote(src, dst, d2_send, sem, e, core1).start()

            @pl.loop(1, 8)
            def _(i):
                d = (b + step_of(i)) % 8
                src, dst, sem = core0_path(d)
                remote(src, dst, d2_send, sem, at(a, d), core0 + half).start()

        @pl.when(core == 1)
        def _():
            src, dst, sem = core1_path(b, 0)
            remote(src, dst, d2_send, sem, e, core0).start()
            src, dst, sem = core1_path(b, 1)
            pltpu.make_async_copy(src, dst, sem).start()

            @pl.loop(1, 8)
            def _(i):
                d = (b + step_of(i)) % 8
                for hf in range(2):
                    src, dst, sem = core1_path(d, hf)
                    remote(src, dst, d2_send, sem, at(a, d), core0 + hf).start()

        sent.append(gone_d2)

    def forward0(p, k):
        arrived(x0.at[p, k], c_send, d2_recv0.at[p, k])
        remote(x0.at[p, k], c0.at[p, k], c_send, c_recv0.at[p, k], e, cross).start()

    def forward1(p, i):
        k = (y + step_of(i)) % 8
        arrived(x1.at[p, k], c_send, d2_recv1.at[p, k])
        remote(x1.at[p, k], c1.at[p, k], c_send, c_recv1.at[p, k], e, cross).start()

    def forward_rest(p):
        @pl.loop(0, 4)
        def _(i):
            forward0(p, i)

            @pl.when(i >= FIRST // 2)
            def _():
                forward1(p, 2 * i)
                forward1(p, 2 * i + 1)

        sent.append(lambda: (left(x0.at[p], c_send, c_recv0.at[p, 0]), left(x1.at[p], c_send, c_recv0.at[p, 0])))

    def forward_first(p):
        @pl.loop(0, FIRST)
        def _(i):
            forward1(p, i)

    def take_c0(p):
        @pl.loop(0, 4)
        def _(i):
            arrived(c0.at[p, i], c_send, c_recv0.at[p, i])

    def take_c1(p):
        @pl.loop(0, 8)
        def _(i):
            arrived(c1.at[p, i], c_send, c_recv1.at[p, i])

    def multiply(values, column, zero=False):
        rows = pl.ds(pl.multiple_of(column, PIECE), PIECE)
        for n in range(2):
            cols = slice(n * PAIR_HIDDEN, n * PAIR_HIDDEN + PAIR_HIDDEN)
            product = lax.dot_general(
                values,
                gate_up[2 * n : 2 * n + 2, :, rows].reshape(PAIR_HIDDEN, PIECE),
                (((1,), (1,)), ((), ())),
                preferred_element_type=F32,
            )
            hidden[:, cols] = product if zero else hidden[:, cols] + product

    def natural(ref, p):
        return ref[p].reshape(ROWS, PIECE)

    def turned(ref, p):
        return jnp.concatenate([ref[p, :, k].reshape(96, PIECE) for k in range(4)], axis=0)

    own, other = side * 1024, (1 - side) * 1024

    dispatch_first(0)
    dispatch_first(1)
    take("pair")
    take("wd cross")
    send(wd.at[2], wd.at[3], wd_send.at[2], wd_recv.at[2], e, partner)
    expect("wd", wd.at[3], wd_send.at[2], wd_recv.at[2])
    dispatch_second(0)
    forward_first(0)
    dispatch_second(1)
    forward_rest(0)
    multiply(natural(x0, 0), own, True)
    multiply(turned(x1, 0), own + QUARTER)
    forward_first(1)
    forward_rest(1)
    take("ring")
    ring_start(1)
    multiply(natural(x0, 1), own + PIECE)
    multiply(turned(x1, 1), own + QUARTER + PIECE)
    take_c0(0)
    multiply(natural(c0, 0), other)
    take_c1(0)
    multiply(turned(c1, 0), other + QUARTER)
    take_c0(1)
    multiply(natural(c0, 1), other + PIECE)
    take_c1(1)
    multiply(turned(c1, 1), other + QUARTER + PIECE)

    gate = hidden[:, 0:PAIR_HIDDEN]
    act[...] = (
        gate * (1.0 / (1.0 + jnp.exp(-gate))) * hidden[:, PAIR_HIDDEN : 2 * PAIR_HIDDEN]
    ).astype(BF)
    send(act, act_in, act_send, act_recv, e, cross)
    take("ring")
    ring_start(2)

    take("wd")
    for n in range(4):
        cols = slice(n * 256, n * 256 + 256)
        y_acc[:, cols] = dot(act[...], wd[0:2, :, cols].reshape(PAIR_HIDDEN, 256))
    arrived(act_in, act_send, act_recv)

    first_zone = 4 * core

    def gone_r3():
        left(y1.at[0, pl.ds(0, 7)], r3_send, r3_recv.at[0])

        @pl.when((core == 0) & (half == 0))
        def _():
            left(y0.at[0, pl.ds(0, 3)], r3_send, r3_recv.at[0])
            left(y1.at[0, 0], r3_send, r3_recv.at[0])

        @pl.when((core == 0) & (half == 1))
        def _():
            left(y0.at[0], r3_send, r3_recv.at[0])
            left(y1.at[0, 0], r3_send, r3_recv.at[0])

        @pl.when(core == 1)
        def _():
            left(y0.at[0], r3_send, r3_recv.at[0])

    for p in range(2):
        for n in (p, 2 + p):
            cols = slice(n * PIECE, n * PIECE + PIECE)
            out = y_acc[:, cols] + dot(act_in[...], wd[2:4, :, cols].reshape(PAIR_HIDDEN, PIECE))
            blocks = out.astype(BF).reshape(4, 8, 3, 4, PIECE)
            if n < 2:
                y0[p] = blocks
            else:
                for k in range(4):
                    y1[p, :, k] = blocks[k]

        @pl.loop(0, 4)
        def _(i):
            zone = first_zone + i
            src, dst = y0.at[p, i], r3.at[p, z]

            @pl.when(zone != z)
            def _():
                remote(src, dst, r3_send, r3_recv.at[p], zone * 8 + y, core0).start()

            @pl.when((zone == z) & (core == 0))
            def _():
                pltpu.make_async_copy(src, dst, r3_recv.at[p]).start()

            @pl.when((zone == z) & (core == 1))
            def _():
                remote(src, dst, r3_send, r3_recv.at[p], e, core0).start()

        into = r3.at[p, y, pl.ds(first_zone, 4)]

        @pl.loop(1, 8)
        def _(i):
            d = (y + step_of(i)) % 8
            remote(y1.at[p, d], into, r3_send, r3_recv.at[p], z * 8 + d, core1).start()

        @pl.when(core == 1)
        def _():
            pltpu.make_async_copy(y1.at[p, y], into, r3_recv.at[p]).start()

        @pl.when(core == 0)
        def _():
            remote(y1.at[p, y], into, r3_send, r3_recv.at[p], e, core1).start()

        sent.append(gone_r3)

    for p in range(2):
        arrived(r3.at[p], r3_send, r3_recv.at[p])

        @pl.loop(1, 8)
        def _(i):
            d = (a + step_of(i)) % 8
            remote(r3.at[p, :, d], r4.at[p, a], r4_send, r4_recv.at[p], at(d, b), t).start()

        pltpu.make_async_copy(r3.at[p, :, a], r4.at[p, a], r4_recv.at[p]).start()
        sent.append(lambda: left(r4.at[0, pl.ds(0, 7)], r4_send, r4_recv.at[0]))

    for p in range(2):
        arrived(r4.at[p], r4_send, r4_recv.at[p])
        returned = r4[p].reshape(SLOTS, PIECE)
        weighted = dot(mix_hi[...], returned) + dot(mix_lo[...], returned)
        sums_out[:, :, p * PIECE : p * PIECE + PIECE] = weighted.astype(BF).reshape(
            8, TOKENS, PIECE
        )
    sums_in[t] = sums_out[t]

    to_tensor("sums", lambda d: sums_out.at[d], sums_in, sums_send, sums_recv)
    take("ring")
    ring_start(3)
    take("sums")

    expert_sum = jnp.concatenate(
        [sums_in[s].astype(F32) + sums_in[s + 4].astype(F32) for s in range(4)], axis=1
    )
    next_residual = (first[...].astype(F32) + expert_sum).astype(BF)
    moved_ref[...] = next_residual
    nx[t] = normalize(next_residual.astype(F32), input_gain[...]).astype(BF)

    for i in (2, 1, 3):
        d = 2 * ((chip + i) % 4) + core
        send(nx.at[t], nx.at[t], nx_send.at[i], nx_recv.at[t], e, d)
    send(nx.at[t], nx.at[t], nx_send.at[0], nx_recv.at[t], e, partner)
    for i in (1, 3, 2):
        s = 2 * ((chip + i) % 4) + core
        arrived(nx.at[s], nx_send.at[i], nx_recv.at[s])
        send(nx.at[s], nx.at[s], nx_send.at[4 + i], nx_recv.at[s], e, partner)

    take("ring")

    for i in range(4):
        s = 2 * ((chip + i) % 4) + 1 - core
        arrived(nx.at[s], nx_send.at[i], nx_recv.at[s])

    tokens = nx[...].reshape(GROUP, D)
    raw = jnp.zeros((GROUP, QKV), F32)
    for zz in range(8):
        blocks = []
        for yy in range(8):
            second = zz + core * (yy - zz)
            blocks.append(qw[second, yy + core * (zz - yy)])
        raw += dot(tokens[:, zz * 256 : zz * 256 + 256], jnp.concatenate(blocks, axis=0))
    raw_ref[...] = raw

    for gone in sent:
        gone()


def finish(moved_ref, raw_ref, q_gain, k_gain, next_ref, queries_ref, kv_ref):
    t = lax.axis_index("tensor")
    next_ref[...] = moved_ref[...]
    for head in range(4):
        cols = slice(head * HEAD, head * HEAD + HEAD)
        queries_ref[:, cols] = normalize(raw_ref[:, cols], q_gain[...]).astype(BF)
    kv_raw = raw_ref[:, 512:QKV]
    kv_ref[...] = jnp.where(t < KV_HEADS, normalize(kv_raw, k_gain[...]), kv_raw).astype(BF)


def per_device(
    attn_out,
    out_weight,
    residual,
    attn_gain,
    expert_ids,
    route_weights,
    w_gate,
    w_up,
    w_down,
    input_gain,
    q_weight,
    kv_weight,
    q_gain,
    k_gain,
):
    any_spec = pl.BlockSpec(memory_space=pl.ANY)
    vmem = pl.BlockSpec(memory_space=pltpu.VMEM)
    dma = pltpu.SemaphoreType.DMA
    rows = (3, 4, PIECE)

    def buf(*shape):
        return pltpu.VMEM(shape, BF)

    moved, raw = pl.pallas_call(
        kernel,
        out_shape=(
            jax.ShapeDtypeStruct((TOKENS, D), BF),
            jax.ShapeDtypeStruct((GROUP, QKV), F32),
        ),
        in_specs=[
            any_spec,
            any_spec,
            vmem,
            vmem,
            vmem,
            vmem,
            any_spec,
            any_spec,
            any_spec,
            vmem,
            any_spec,
            any_spec,
        ],
        out_specs=(vmem, vmem),
        scratch_shapes=[
            buf(GROUP, 512),
            buf(512, D),
            buf(4, HIDDEN, D),
            buf(HIDDEN, D),
            buf(4, HIDDEN, D // 2),
            buf(8, 8, 32, QKV),
            buf(8, TOKENS, D),
            buf(4, TOKENS, D),
            buf(4, TOKENS, D),
            buf(4, TOKENS, D),
            buf(4, TOKENS, QUARTER),
            buf(8, TOKENS, QUARTER),
            buf(SLOTS, GROUP),
            buf(GROUP, SLOTS),
            buf(GROUP, SLOTS),
            buf(2, 8, 8, *rows),
            buf(2, 8, 8, *rows),
            buf(2, 4, 8, *rows),
            buf(2, 8, 4, *rows),
            buf(2, 4, 8, *rows),
            buf(2, 8, 4, *rows),
            pltpu.VMEM((ROWS, 2 * PAIR_HIDDEN), F32),
            buf(ROWS, PAIR_HIDDEN),
            buf(ROWS, PAIR_HIDDEN),
            pltpu.VMEM((ROWS, D // 2), F32),
            buf(2, 4, 8, *rows),
            buf(2, 8, 4, *rows),
            buf(2, 8, 8, *rows),
            buf(2, 8, 8, *rows),
            buf(8, TOKENS, QUARTER),
            buf(8, TOKENS, QUARTER),
            buf(TOKENS, D),
            buf(8, TOKENS, D),
            dma((10,)),
            dma((4,)),
            dma((4,)),
            dma((4,)),
            dma((4,)),
            dma((8,)),
            dma((8,)),
            dma((2,)),
            dma((2,)),
            dma((3,)),
            dma((3,)),
            dma((8,)),
            dma((8,)),
            dma((4, 2)),
            dma((4, 2)),
            dma,
            dma((2,)),
            dma,
            dma((2, 4)),
            dma((2, 8)),
            dma,
            dma((2, 4)),
            dma((2, 8)),
            dma,
            dma,
            dma,
            dma((2,)),
            dma,
            dma((2,)),
            dma((8,)),
            dma((8,)),
            dma((8,)),
            dma((8,)),
        ],
        compiler_params=pltpu.CompilerParams(
            collective_id=0, has_side_effects=True, vmem_limit_bytes=66_400_000
        ),
    )(
        attn_out,
        out_weight,
        residual,
        attn_gain.reshape(1, -1),
        expert_ids.T,
        route_weights.T,
        jnp.swapaxes(w_gate, 1, 2),
        jnp.swapaxes(w_up, 1, 2),
        w_down,
        input_gain.reshape(1, -1),
        q_weight,
        kv_weight,
    )
    return pl.pallas_call(
        finish,
        out_shape=(
            jax.ShapeDtypeStruct((TOKENS, D), BF),
            jax.ShapeDtypeStruct((GROUP, 512), BF),
            jax.ShapeDtypeStruct((GROUP, HEAD), BF),
        ),
        in_specs=[vmem] * 4,
        out_specs=(vmem, vmem, vmem),
        compiler_params=pltpu.CompilerParams(vmem_limit_bytes=66_400_000),
    )(moved, raw, q_gain.reshape(1, -1), k_gain.reshape(1, -1))


def solution(mesh):
    return jax.shard_map(
        per_device,
        mesh=mesh,
        in_specs=(
            P("expert", "tensor"),
            P("tensor", None),
            P(("expert", "tensor"), None),
            P(),
            P("expert", None),
            P("expert", None),
            P("expert", None, "tensor"),
            P("expert", None, "tensor"),
            P("expert", "tensor", None),
            P(),
            P("expert", "tensor"),
            P("expert", "tensor"),
            P(),
            P(),
        ),
        out_specs=(P(("expert", "tensor"), None), P("expert", "tensor"), P("expert", "tensor")),
        check_vma=False,
    )
```

```python
import jax
import jax.numpy as jnp
from jax import lax
from jax.experimental import pallas as pl
from jax.experimental.pallas import tpu as pltpu
from jax.sharding import PartitionSpec as P

MESH = pl.DeviceIdType.MESH
BF = jnp.bfloat16
F32 = jnp.float32

KV_HEADS = 4
TOP = 8
EPSILON = 1e-06

D = 2048
GROUP = 128
TOKENS = 16
CAP = 12
QUARTER = 512
PIECE = 256
FIRST = 4
HIDDEN = 192
PAIR_HIDDEN = 384
ROWS = 384
SLOTS = 768
QKV = 640
HEAD = 128


def normalize(values, gain):
    return values * lax.rsqrt(jnp.mean(values * values, axis=-1, keepdims=True) + EPSILON) * gain


def dot(a, b):
    return jnp.dot(a, b, preferred_element_type=F32)


def iota(shape, axis):
    return lax.broadcasted_iota(jnp.int32, shape, axis)


def kernel(
    attn_hbm,
    ow_hbm,
    res_ref,
    attn_gain,
    ids_ref,
    rw_ref,
    wg_hbm,
    wu_hbm,
    wd_hbm,
    input_gain,
    qw_hbm,
    kvw_hbm,
    moved_ref,
    raw_ref,
    attn,
    ow,
    gate_up,
    wd_own,
    wd,
    qw,
    partial,
    mates,
    sums_of_chip,
    rs_in,
    normed_out,
    normed_in,
    pick,
    mix_hi,
    mix_lo,
    tx,
    r1,
    x0,
    x1,
    c0,
    c1,
    hidden,
    act,
    act_in,
    y_acc,
    y0,
    y1,
    r3,
    r4,
    sums_out,
    sums_in,
    first,
    nx,
    load_sem,
    mate_send,
    mate_recv,
    rs_send,
    rs_recv,
    nb_send,
    nb_recv,
    pair_send,
    pair_recv,
    wd_send,
    wd_recv,
    q1_send,
    q1_recv,
    q2_send,
    q2_recv,
    d1_send,
    d1_recv,
    d2_send,
    d2_recv0,
    d2_recv1,
    c_send,
    c_recv0,
    c_recv1,
    act_send,
    act_recv,
    r3_send,
    r3_recv,
    r4_send,
    r4_recv,
    sums_send,
    sums_recv,
    nx_send,
    nx_recv,
):
    e = lax.axis_index("expert")
    t = lax.axis_index("tensor")
    z, y = e // 8, e % 8
    core = t % 2
    side = (t // 2) % 2
    parity = t // 4
    chip = t // 2
    partner = t + 1 - 2 * core
    cross = t + 2 - 4 * side
    core0, core1 = t - core, t - core + 1
    half = z // 4
    a = y + core * (z - y)
    b = z + core * (y - z)

    def at(first_axis, second_axis):
        return (second_axis + core * (first_axis - second_axis)) * 8 + (
            first_axis + core * (second_axis - first_axis)
        )

    def step_of(i):
        return jnp.where(i % 2 == 1, (i + 1) // 2, 8 - i // 2)

    def far_first(i):
        return jnp.where(i % 2 == 1, 4 + (i - 1) // 2, 4 - i // 2)

    def remote(src, dst, send, recv, expert, tensor):
        return pltpu.make_async_remote_copy(
            src_ref=src,
            dst_ref=dst,
            send_sem=send,
            recv_sem=recv,
            device_id={"expert": expert, "tensor": tensor},
            device_id_type=MESH,
        )

    def arrived(dst, send, recv):
        remote(dst, dst, send, recv, e, partner).wait_recv()

    def left(src, send, recv):
        remote(src, src, send, recv, e, partner).wait_send()

    sent, coming = [], {}

    def send(src, dst, send_sem, recv_sem, expert, tensor):
        remote(src, dst, send_sem, recv_sem, expert, tensor).start()
        sent.append(lambda: left(src, send_sem, recv_sem))

    def expect(name, dst, send_sem, recv_sem):
        coming.setdefault(name, []).append(lambda: arrived(dst, send_sem, recv_sem))

    def take(name):
        for wait in coming.pop(name):
            wait()

    def to_tensor(name, src_of, dst, send_sem, recv_sem):
        @pl.loop(1, 8)
        def _(i):
            d = (t + i) % 8
            remote(src_of(d), dst.at[t], send_sem.at[d], recv_sem.at[t], e, d).start()

        def waits():
            @pl.loop(1, 8)
            def _(i):
                s = (t + i) % 8
                arrived(dst.at[s], send_sem.at[s], recv_sem.at[s])

        def gone():
            @pl.loop(1, 8)
            def _(i):
                d = (t + i) % 8
                left(src_of(d), send_sem.at[d], recv_sem.at[d])

        coming[name] = [waits]
        sent.append(gone)

    barrier = pltpu.get_barrier_semaphore()

    @pl.loop(1, 8)
    def _(i):
        pl.semaphore_signal(
            barrier, inc=1, device_id={"expert": e, "tensor": (t + i) % 8}, device_id_type=MESH
        )
        for which in (core0, core1):
            pl.semaphore_signal(
                barrier,
                inc=1,
                device_id={"expert": z * 8 + (y + i) % 8, "tensor": which},
                device_id_type=MESH,
            )
            pl.semaphore_signal(
                barrier,
                inc=1,
                device_id={"expert": ((z + i) % 8) * 8 + y, "tensor": which},
                device_id_type=MESH,
            )

    ow_parts = [
        pltpu.make_async_copy(
            ow_hbm.at[:, pl.ds(n * 512, 512)], ow.at[:, pl.ds(n * 512, 512)], load_sem.at[6 + n]
        )
        for n in range(4)
    ]
    loads = [
        pltpu.make_async_copy(attn_hbm, attn, load_sem.at[0]),
        pltpu.make_async_copy(qw_hbm, qw.at[b, a, :, pl.ds(0, 512)], load_sem.at[1]),
        pltpu.make_async_copy(kvw_hbm, qw.at[b, a, :, pl.ds(512, 128)], load_sem.at[2]),
        pltpu.make_async_copy(wg_hbm.at[0], gate_up.at[0], load_sem.at[3]),
        pltpu.make_async_copy(wu_hbm.at[0], gate_up.at[2], load_sem.at[4]),
        pltpu.make_async_copy(wd_hbm.at[0], wd_own, load_sem.at[5]),
    ]
    loads[0].start()
    for part in ow_parts:
        part.start()
    for load in loads[1:]:
        load.start()

    loads[0].wait()
    for n in range(4):
        ow_parts[n].wait()
        cols = slice(n * 512, n * 512 + 512)
        partial[:, :, cols] = dot(attn[...], ow[:, cols]).astype(BF).reshape(8, TOKENS, 512)

    pl.semaphore_wait(barrier, 35)

    for k in range(4):
        theirs = 2 * k + 1 - core
        send(partial.at[theirs], mates.at[k], mate_send.at[k], mate_recv.at[k], e, partner)

    def chip_sum(k):
        arrived(mates.at[k], mate_send.at[k], mate_recv.at[k])
        return (partial[2 * k + core].astype(F32) + mates[k].astype(F32)).astype(BF)

    for i in (2, 1, 3):
        k = (chip + i) % 4
        sums_of_chip[k] = chip_sum(k)
        send(sums_of_chip.at[k], rs_in.at[chip], rs_send.at[k], rs_recv.at[chip], e, 2 * k + core)
        expect("rs", rs_in.at[k], rs_send.at[k], rs_recv.at[k])
    rs_in[chip] = chip_sum(chip)

    loads[1].wait()
    loads[2].wait()

    @pl.loop(1, 8)
    def _(i):
        d = (a + step_of(i)) % 8
        remote(
            qw.at[b, a], qw.at[b, a], q1_send.at[d], q1_recv.at[a], at(d, b), t
        ).start()

    def q1_left():
        @pl.loop(1, 8)
        def _(i):
            n = (a + i) % 8
            left(qw.at[b, a], q1_send.at[n], q1_recv.at[n])

    sent.append(q1_left)

    loads[3].wait()
    loads[4].wait()
    for k in range(2):
        send(gate_up.at[2 * k], gate_up.at[2 * k + 1], pair_send.at[k], pair_recv.at[k], e, partner)
        expect("pair", gate_up.at[2 * k + 1], pair_send.at[k], pair_recv.at[k])

    position = iota((GROUP, 64), 1)
    p_first, p_second = position // 8, position % 8
    expert_of = 2 * at(p_first, p_second) + parity
    ids = ids_ref[...].T
    weights = rw_ref[...].T
    named = jnp.zeros((GROUP, 64), F32)
    weight_of = jnp.zeros((GROUP, 64), F32)
    for k in range(TOP):
        hit = expert_of == ids[:, k : k + 1]
        named += jnp.where(hit, 1.0, 0.0)
        weight_of += jnp.where(hit, weights[:, k : k + 1], 0.0)
    lower = jnp.where(iota((GROUP, GROUP), 1) < iota((GROUP, GROUP), 0), 1.0, 0.0).astype(BF)
    rank = dot(lower, named.astype(BF))
    code = (named * (rank + 1.0)).astype(BF)
    slot = iota((64, SLOTS), 1)
    start = iota((64, SLOTS), 0) * CAP
    spread = jnp.where((slot >= start) & (slot < start + CAP), 1.0, 0.0).astype(BF)
    wanted = (iota((GROUP, SLOTS), 1) % CAP + 1).astype(F32)
    chosen = dot(code, spread) == wanted
    high = weight_of.astype(BF)
    low = (weight_of - high.astype(F32)).astype(BF)
    mix_hi[...] = jnp.where(chosen, dot(high, spread), 0.0).astype(BF)
    mix_lo[...] = jnp.where(chosen, dot(low, spread), 0.0).astype(BF)
    pick[...] = jnp.where(chosen, 1.0, 0.0).T.astype(BF)

    after, before = at(a, (b + 1) % 8), at(a, (b + 7) % 8)

    def ring(step):
        rows = ((b + 8 - step) % 8, (b + step) % 8)
        if step == 3:
            pieces = (qw.at[rows[0], pl.ds(0, 4)], qw.at[rows[1], pl.ds(4, 4)])
        else:
            pieces = (qw.at[rows[0]], qw.at[rows[1]])
        return [
            remote(pieces[k], pieces[k], q2_send.at[step, k], q2_recv.at[step, k], (after, before)[k], t)
            for k in range(2)
        ]

    def ring_wait(step):
        rows = ((b + 7 - step) % 8, (b + 1 + step) % 8)
        if step == 3:
            pieces = (qw.at[rows[0], pl.ds(0, 4)], qw.at[rows[1], pl.ds(4, 4)])
        else:
            pieces = (qw.at[rows[0]], qw.at[rows[1]])
        for k in range(2):
            arrived(pieces[k], q2_send.at[step, k], q2_recv.at[step, k])

    @pl.loop(1, 8)
    def _(i):
        s = (a + i) % 8
        arrived(qw.at[b, s], q1_send.at[s], q1_recv.at[s])

    def ring_start(step):
        for c in ring(step):
            c.start()
        sent.append(lambda: [c.wait_send() for c in ring(step)])
        coming["ring"] = [lambda: ring_wait(step)]

    ring_start(0)

    take("rs")

    total = res_ref[...].astype(F32)
    attn_sum = rs_in[0].astype(F32)
    for k in range(1, 4):
        attn_sum += rs_in[k].astype(F32)
    first_residual = (total + attn_sum).astype(BF)
    first[...] = first_residual
    normed = normalize(first_residual.astype(F32), attn_gain[...]).astype(BF)
    for s in range(4):
        normed_out[s] = normed[:, s * QUARTER : s * QUARTER + QUARTER]
    normed_in[t] = normed_out[t % 4]

    to_tensor("nb", lambda d: normed_out.at[d % 4], normed_in, nb_send, nb_recv)

    loads[5].wait()
    own_half = pl.ds(pl.multiple_of(side * 1024, 1024), 1024)
    other_half = pl.ds(pl.multiple_of((1 - side) * 1024, 1024), 1024)
    send(wd_own.at[:, own_half], wd.at[1], wd_send.at[0], wd_recv.at[0], e, partner)
    expect("wd", wd.at[1], wd_send.at[0], wd_recv.at[0])
    send(wd_own.at[:, other_half], wd.at[2], wd_send.at[1], wd_recv.at[1], e, cross)
    expect("wd cross", wd.at[2], wd_send.at[1], wd_recv.at[1])
    wd[0] = wd_own[:, own_half]

    take("nb")

    group = normed_in[...].reshape(GROUP, QUARTER)

    def gone_d2():
        @pl.when(core == 0)
        def _():
            left(r1.at[0, pl.ds(0, 7)], d2_send, d2_recv0.at[0, 0])

            @pl.when(half == 1)
            def _():
                left(r1.at[0, 0], d2_send, d2_recv0.at[0, 0])

        @pl.when(core == 1)
        def _():
            left(r1.at[0, pl.ds(0, 7)], d2_send, d2_recv0.at[0, 0])
            left(r1.at[0, 0, pl.ds(0, 4)], d2_send, d2_recv0.at[0, 0])

    def dispatch_first(p):
        for k in range(2):
            rows = slice(k * 384, k * 384 + 384)
            tx[p, 4 * k : 4 * k + 4] = (
                dot(pick[rows, :], group[:, p * PIECE : p * PIECE + PIECE])
                .astype(BF)
                .reshape(4, 8, 3, 4, PIECE)
            )

        @pl.loop(1, 8)
        def _(i):
            d = (a + far_first(i)) % 8
            remote(tx.at[p, d], r1.at[p, a], d1_send, d1_recv.at[p], at(d, b), t).start()

        pltpu.make_async_copy(tx.at[p, a], r1.at[p, a], d1_recv.at[p]).start()
        sent.append(lambda: left(tx.at[p, pl.ds(0, 7)], d1_send, d1_recv.at[p]))

    def dispatch_second(p):
        arrived(r1.at[p], d1_send, d1_recv.at[p])

        def core0_path(d):
            return r1.at[p, :, d], x0.at[p, z % 4], d2_recv0.at[p, z % 4]

        def core1_path(d, hf):
            return r1.at[p, pl.ds(4 * hf, 4), d], x1.at[p, y], d2_recv1.at[p, y]

        @pl.when(core == 0)
        def _():
            src, dst, sem = core0_path(b)

            @pl.when(half == 0)
            def _():
                pltpu.make_async_copy(src, dst, sem).start()

            @pl.when(half == 1)
            def _():
                remote(src, dst, d2_send, sem, e, core1).start()

            @pl.loop(1, 8)
            def _(i):
                d = (b + step_of(i)) % 8
                src, dst, sem = core0_path(d)
                remote(src, dst, d2_send, sem, at(a, d), core0 + half).start()

        @pl.when(core == 1)
        def _():
            src, dst, sem = core1_path(b, 0)
            remote(src, dst, d2_send, sem, e, core0).start()
            src, dst, sem = core1_path(b, 1)
            pltpu.make_async_copy(src, dst, sem).start()

            @pl.loop(1, 8)
            def _(i):
                d = (b + step_of(i)) % 8
                for hf in range(2):
                    src, dst, sem = core1_path(d, hf)
                    remote(src, dst, d2_send, sem, at(a, d), core0 + hf).start()

        sent.append(gone_d2)

    def forward0(p, k):
        arrived(x0.at[p, k], c_send, d2_recv0.at[p, k])
        remote(x0.at[p, k], c0.at[p, k], c_send, c_recv0.at[p, k], e, cross).start()

    def forward1(p, i):
        k = (y + step_of(i)) % 8
        arrived(x1.at[p, k], c_send, d2_recv1.at[p, k])
        remote(x1.at[p, k], c1.at[p, k], c_send, c_recv1.at[p, k], e, cross).start()

    def forward_rest(p):
        @pl.loop(0, 4)
        def _(i):
            forward0(p, i)

            @pl.when(i >= FIRST // 2)
            def _():
                forward1(p, 2 * i)
                forward1(p, 2 * i + 1)

        sent.append(lambda: (left(x0.at[p], c_send, c_recv0.at[p, 0]), left(x1.at[p], c_send, c_recv0.at[p, 0])))

    def forward_first(p):
        @pl.loop(0, FIRST)
        def _(i):
            forward1(p, i)

    def take_c0(p):
        @pl.loop(0, 4)
        def _(i):
            arrived(c0.at[p, i], c_send, c_recv0.at[p, i])

    def take_c1(p):
        @pl.loop(0, 8)
        def _(i):
            arrived(c1.at[p, i], c_send, c_recv1.at[p, i])

    def multiply(values, column, zero=False):
        rows = pl.ds(pl.multiple_of(column, PIECE), PIECE)
        for n in range(2):
            cols = slice(n * PAIR_HIDDEN, n * PAIR_HIDDEN + PAIR_HIDDEN)
            product = lax.dot_general(
                values,
                gate_up[2 * n : 2 * n + 2, :, rows].reshape(PAIR_HIDDEN, PIECE),
                (((1,), (1,)), ((), ())),
                preferred_element_type=F32,
            )
            hidden[:, cols] = product if zero else hidden[:, cols] + product

    def natural(ref, p):
        return ref[p].reshape(ROWS, PIECE)

    def turned(ref, p):
        return jnp.concatenate([ref[p, :, k].reshape(96, PIECE) for k in range(4)], axis=0)

    own, other = side * 1024, (1 - side) * 1024

    dispatch_first(0)
    dispatch_first(1)
    take("pair")
    take("wd cross")
    send(wd.at[2], wd.at[3], wd_send.at[2], wd_recv.at[2], e, partner)
    expect("wd", wd.at[3], wd_send.at[2], wd_recv.at[2])
    dispatch_second(0)
    forward_first(0)
    dispatch_second(1)
    forward_rest(0)
    multiply(natural(x0, 0), own, True)
    multiply(turned(x1, 0), own + QUARTER)
    forward_first(1)
    forward_rest(1)
    take("ring")
    ring_start(1)
    multiply(natural(x0, 1), own + PIECE)
    multiply(turned(x1, 1), own + QUARTER + PIECE)
    take_c0(0)
    multiply(natural(c0, 0), other)
    take_c1(0)
    multiply(turned(c1, 0), other + QUARTER)
    take_c0(1)
    multiply(natural(c0, 1), other + PIECE)
    take_c1(1)
    multiply(turned(c1, 1), other + QUARTER + PIECE)

    gate = hidden[:, 0:PAIR_HIDDEN]
    act[...] = (
        gate * (1.0 / (1.0 + jnp.exp(-gate))) * hidden[:, PAIR_HIDDEN : 2 * PAIR_HIDDEN]
    ).astype(BF)
    send(act, act_in, act_send, act_recv, e, cross)
    take("ring")
    ring_start(2)

    take("wd")
    for n in range(4):
        cols = slice(n * 256, n * 256 + 256)
        y_acc[:, cols] = dot(act[...], wd[0:2, :, cols].reshape(PAIR_HIDDEN, 256))
    arrived(act_in, act_send, act_recv)

    first_zone = 4 * core

    def gone_r3():
        left(y1.at[0, pl.ds(0, 7)], r3_send, r3_recv.at[0])

        @pl.when((core == 0) & (half == 0))
        def _():
            left(y0.at[0, pl.ds(0, 3)], r3_send, r3_recv.at[0])
            left(y1.at[0, 0], r3_send, r3_recv.at[0])

        @pl.when((core == 0) & (half == 1))
        def _():
            left(y0.at[0], r3_send, r3_recv.at[0])
            left(y1.at[0, 0], r3_send, r3_recv.at[0])

        @pl.when(core == 1)
        def _():
            left(y0.at[0], r3_send, r3_recv.at[0])

    for p in range(2):
        for n in (p, 2 + p):
            cols = slice(n * PIECE, n * PIECE + PIECE)
            out = y_acc[:, cols] + dot(act_in[...], wd[2:4, :, cols].reshape(PAIR_HIDDEN, PIECE))
            blocks = out.astype(BF).reshape(4, 8, 3, 4, PIECE)
            if n < 2:
                y0[p] = blocks
            else:
                for k in range(4):
                    y1[p, :, k] = blocks[k]

        @pl.loop(0, 4)
        def _(i):
            zone = first_zone + i
            src, dst = y0.at[p, i], r3.at[p, z]

            @pl.when(zone != z)
            def _():
                remote(src, dst, r3_send, r3_recv.at[p], zone * 8 + y, core0).start()

            @pl.when((zone == z) & (core == 0))
            def _():
                pltpu.make_async_copy(src, dst, r3_recv.at[p]).start()

            @pl.when((zone == z) & (core == 1))
            def _():
                remote(src, dst, r3_send, r3_recv.at[p], e, core0).start()

        into = r3.at[p, y, pl.ds(first_zone, 4)]

        @pl.loop(1, 8)
        def _(i):
            d = (y + far_first(i)) % 8
            remote(y1.at[p, d], into, r3_send, r3_recv.at[p], z * 8 + d, core1).start()

        @pl.when(core == 1)
        def _():
            pltpu.make_async_copy(y1.at[p, y], into, r3_recv.at[p]).start()

        @pl.when(core == 0)
        def _():
            remote(y1.at[p, y], into, r3_send, r3_recv.at[p], e, core1).start()

        sent.append(gone_r3)

    for p in range(2):
        arrived(r3.at[p], r3_send, r3_recv.at[p])

        @pl.loop(1, 8)
        def _(i):
            d = (a + far_first(i)) % 8
            remote(r3.at[p, :, d], r4.at[p, a], r4_send, r4_recv.at[p], at(d, b), t).start()

        pltpu.make_async_copy(r3.at[p, :, a], r4.at[p, a], r4_recv.at[p]).start()
        sent.append(lambda: left(r4.at[0, pl.ds(0, 7)], r4_send, r4_recv.at[0]))

    for p in range(2):
        arrived(r4.at[p], r4_send, r4_recv.at[p])
        returned = r4[p].reshape(SLOTS, PIECE)
        weighted = dot(mix_hi[...], returned) + dot(mix_lo[...], returned)
        sums_out[:, :, p * PIECE : p * PIECE + PIECE] = weighted.astype(BF).reshape(
            8, TOKENS, PIECE
        )
    sums_in[t] = sums_out[t]

    to_tensor("sums", lambda d: sums_out.at[d], sums_in, sums_send, sums_recv)
    take("ring")
    ring_start(3)
    take("sums")

    expert_sum = jnp.concatenate(
        [sums_in[s].astype(F32) + sums_in[s + 4].astype(F32) for s in range(4)], axis=1
    )
    next_residual = (first[...].astype(F32) + expert_sum).astype(BF)
    moved_ref[...] = next_residual
    nx[t] = normalize(next_residual.astype(F32), input_gain[...]).astype(BF)

    for i in (2, 1, 3):
        d = 2 * ((chip + i) % 4) + core
        send(nx.at[t], nx.at[t], nx_send.at[i], nx_recv.at[t], e, d)
    send(nx.at[t], nx.at[t], nx_send.at[0], nx_recv.at[t], e, partner)
    for i in (1, 3, 2):
        s = 2 * ((chip + i) % 4) + core
        arrived(nx.at[s], nx_send.at[i], nx_recv.at[s])
        send(nx.at[s], nx.at[s], nx_send.at[4 + i], nx_recv.at[s], e, partner)

    take("ring")

    for i in range(4):
        s = 2 * ((chip + i) % 4) + 1 - core
        arrived(nx.at[s], nx_send.at[i], nx_recv.at[s])

    tokens = nx[...].reshape(GROUP, D)
    raw = jnp.zeros((GROUP, QKV), F32)
    for zz in range(8):
        blocks = []
        for yy in range(8):
            second = zz + core * (yy - zz)
            blocks.append(qw[second, yy + core * (zz - yy)])
        raw += dot(tokens[:, zz * 256 : zz * 256 + 256], jnp.concatenate(blocks, axis=0))
    raw_ref[...] = raw

    for gone in sent:
        gone()


def finish(moved_ref, raw_ref, q_gain, k_gain, next_ref, queries_ref, kv_ref):
    t = lax.axis_index("tensor")
    next_ref[...] = moved_ref[...]
    for head in range(4):
        cols = slice(head * HEAD, head * HEAD + HEAD)
        queries_ref[:, cols] = normalize(raw_ref[:, cols], q_gain[...]).astype(BF)
    kv_raw = raw_ref[:, 512:QKV]
    kv_ref[...] = jnp.where(t < KV_HEADS, normalize(kv_raw, k_gain[...]), kv_raw).astype(BF)


def per_device(
    attn_out,
    out_weight,
    residual,
    attn_gain,
    expert_ids,
    route_weights,
    w_gate,
    w_up,
    w_down,
    input_gain,
    q_weight,
    kv_weight,
    q_gain,
    k_gain,
):
    any_spec = pl.BlockSpec(memory_space=pl.ANY)
    vmem = pl.BlockSpec(memory_space=pltpu.VMEM)
    dma = pltpu.SemaphoreType.DMA
    rows = (3, 4, PIECE)

    def buf(*shape):
        return pltpu.VMEM(shape, BF)

    moved, raw = pl.pallas_call(
        kernel,
        out_shape=(
            jax.ShapeDtypeStruct((TOKENS, D), BF),
            jax.ShapeDtypeStruct((GROUP, QKV), F32),
        ),
        in_specs=[
            any_spec,
            any_spec,
            vmem,
            vmem,
            vmem,
            vmem,
            any_spec,
            any_spec,
            any_spec,
            vmem,
            any_spec,
            any_spec,
        ],
        out_specs=(vmem, vmem),
        scratch_shapes=[
            buf(GROUP, 512),
            buf(512, D),
            buf(4, HIDDEN, D),
            buf(HIDDEN, D),
            buf(4, HIDDEN, D // 2),
            buf(8, 8, 32, QKV),
            buf(8, TOKENS, D),
            buf(4, TOKENS, D),
            buf(4, TOKENS, D),
            buf(4, TOKENS, D),
            buf(4, TOKENS, QUARTER),
            buf(8, TOKENS, QUARTER),
            buf(SLOTS, GROUP),
            buf(GROUP, SLOTS),
            buf(GROUP, SLOTS),
            buf(2, 8, 8, *rows),
            buf(2, 8, 8, *rows),
            buf(2, 4, 8, *rows),
            buf(2, 8, 4, *rows),
            buf(2, 4, 8, *rows),
            buf(2, 8, 4, *rows),
            pltpu.VMEM((ROWS, 2 * PAIR_HIDDEN), F32),
            buf(ROWS, PAIR_HIDDEN),
            buf(ROWS, PAIR_HIDDEN),
            pltpu.VMEM((ROWS, D // 2), F32),
            buf(2, 4, 8, *rows),
            buf(2, 8, 4, *rows),
            buf(2, 8, 8, *rows),
            buf(2, 8, 8, *rows),
            buf(8, TOKENS, QUARTER),
            buf(8, TOKENS, QUARTER),
            buf(TOKENS, D),
            buf(8, TOKENS, D),
            dma((10,)),
            dma((4,)),
            dma((4,)),
            dma((4,)),
            dma((4,)),
            dma((8,)),
            dma((8,)),
            dma((2,)),
            dma((2,)),
            dma((3,)),
            dma((3,)),
            dma((8,)),
            dma((8,)),
            dma((4, 2)),
            dma((4, 2)),
            dma,
            dma((2,)),
            dma,
            dma((2, 4)),
            dma((2, 8)),
            dma,
            dma((2, 4)),
            dma((2, 8)),
            dma,
            dma,
            dma,
            dma((2,)),
            dma,
            dma((2,)),
            dma((8,)),
            dma((8,)),
            dma((8,)),
            dma((8,)),
        ],
        compiler_params=pltpu.CompilerParams(
            collective_id=0, has_side_effects=True, vmem_limit_bytes=66_400_000
        ),
    )(
        attn_out,
        out_weight,
        residual,
        attn_gain.reshape(1, -1),
        expert_ids.T,
        route_weights.T,
        jnp.swapaxes(w_gate, 1, 2),
        jnp.swapaxes(w_up, 1, 2),
        w_down,
        input_gain.reshape(1, -1),
        q_weight,
        kv_weight,
    )
    return pl.pallas_call(
        finish,
        out_shape=(
            jax.ShapeDtypeStruct((TOKENS, D), BF),
            jax.ShapeDtypeStruct((GROUP, 512), BF),
            jax.ShapeDtypeStruct((GROUP, HEAD), BF),
        ),
        in_specs=[vmem] * 4,
        out_specs=(vmem, vmem, vmem),
        compiler_params=pltpu.CompilerParams(vmem_limit_bytes=66_400_000),
    )(moved, raw, q_gain.reshape(1, -1), k_gain.reshape(1, -1))


def solution(mesh):
    return jax.shard_map(
        per_device,
        mesh=mesh,
        in_specs=(
            P("expert", "tensor"),
            P("tensor", None),
            P(("expert", "tensor"), None),
            P(),
            P("expert", None),
            P("expert", None),
            P("expert", None, "tensor"),
            P("expert", None, "tensor"),
            P("expert", "tensor", None),
            P(),
            P("expert", "tensor"),
            P("expert", "tensor"),
            P(),
            P(),
        ),
        out_specs=(P(("expert", "tensor"), None), P("expert", "tensor"), P("expert", "tensor")),
        check_vma=False,
    )
```

```python
import jax
import jax.numpy as jnp
from jax import lax
from jax.experimental import pallas as pl
from jax.experimental.pallas import tpu as pltpu
from jax.sharding import PartitionSpec as P

MESH = pl.DeviceIdType.MESH
BF = jnp.bfloat16
F32 = jnp.float32

KV_HEADS = 4
TOP = 8
EPSILON = 1e-06

D = 2048
GROUP = 128
TOKENS = 16
CAP = 12
QUARTER = 512
PIECE = 256
FIRST = 4
HIDDEN = 192
PAIR_HIDDEN = 384
ROWS = 384
SLOTS = 768
QKV = 640
HEAD = 128


def normalize(values, gain):
    return values * lax.rsqrt(jnp.mean(values * values, axis=-1, keepdims=True) + EPSILON) * gain


def dot(a, b):
    return jnp.dot(a, b, preferred_element_type=F32)


def iota(shape, axis):
    return lax.broadcasted_iota(jnp.int32, shape, axis)


def kernel(
    attn_hbm,
    ow_hbm,
    res_ref,
    attn_gain,
    ids_ref,
    rw_ref,
    wg_hbm,
    wu_hbm,
    wd_hbm,
    input_gain,
    qw_hbm,
    kvw_hbm,
    moved_ref,
    raw_ref,
    attn,
    ow,
    gate_up,
    wd_own,
    wd,
    qw,
    partial,
    mates,
    sums_of_chip,
    rs_in,
    normed_out,
    normed_in,
    pick,
    mix_hi,
    mix_lo,
    tx,
    r1,
    x0,
    x1,
    c0,
    c1,
    hidden,
    act,
    act_in,
    y_acc,
    y0,
    y1,
    r3,
    r4,
    sums_out,
    sums_in,
    first,
    nx,
    load_sem,
    mate_send,
    mate_recv,
    rs_send,
    rs_recv,
    nb_send,
    nb_recv,
    pair_send,
    pair_recv,
    wd_send,
    wd_recv,
    q1_send,
    q1_recv,
    q2_send,
    q2_recv,
    d1_send,
    d1_recv,
    d2_send,
    d2_recv0,
    d2_recv1,
    c_send,
    c_recv0,
    c_recv1,
    act_send,
    act_recv,
    r3_send,
    r3_recv,
    r4_send,
    r4_recv,
    sums_send,
    sums_recv,
    nx_send,
    nx_recv,
):
    e = lax.axis_index("expert")
    t = lax.axis_index("tensor")
    z, y = e // 8, e % 8
    core = t % 2
    side = (t // 2) % 2
    parity = t // 4
    chip = t // 2
    partner = t + 1 - 2 * core
    cross = t + 2 - 4 * side
    core0, core1 = t - core, t - core + 1
    half = z // 4
    a = y + core * (z - y)
    b = z + core * (y - z)

    def at(first_axis, second_axis):
        return (second_axis + core * (first_axis - second_axis)) * 8 + (
            first_axis + core * (second_axis - first_axis)
        )

    def step_of(i):
        return jnp.where(i % 2 == 1, (i + 1) // 2, 8 - i // 2)

    def remote(src, dst, send, recv, expert, tensor):
        return pltpu.make_async_remote_copy(
            src_ref=src,
            dst_ref=dst,
            send_sem=send,
            recv_sem=recv,
            device_id={"expert": expert, "tensor": tensor},
            device_id_type=MESH,
        )

    def arrived(dst, send, recv):
        remote(dst, dst, send, recv, e, partner).wait_recv()

    def left(src, send, recv):
        remote(src, src, send, recv, e, partner).wait_send()

    sent, coming = [], {}

    def send(src, dst, send_sem, recv_sem, expert, tensor):
        remote(src, dst, send_sem, recv_sem, expert, tensor).start()
        sent.append(lambda: left(src, send_sem, recv_sem))

    def expect(name, dst, send_sem, recv_sem):
        coming.setdefault(name, []).append(lambda: arrived(dst, send_sem, recv_sem))

    def take(name):
        for wait in coming.pop(name):
            wait()

    def to_tensor(name, src_of, dst, send_sem, recv_sem):
        @pl.loop(1, 8)
        def _(i):
            d = (t + i) % 8
            remote(src_of(d), dst.at[t], send_sem.at[d], recv_sem.at[t], e, d).start()

        def waits():
            @pl.loop(1, 8)
            def _(i):
                s = (t + i) % 8
                arrived(dst.at[s], send_sem.at[s], recv_sem.at[s])

        def gone():
            @pl.loop(1, 8)
            def _(i):
                d = (t + i) % 8
                left(src_of(d), send_sem.at[d], recv_sem.at[d])

        coming[name] = [waits]
        sent.append(gone)

    barrier = pltpu.get_barrier_semaphore()

    @pl.loop(1, 8)
    def _(i):
        pl.semaphore_signal(
            barrier, inc=1, device_id={"expert": e, "tensor": (t + i) % 8}, device_id_type=MESH
        )
        for which in (core0, core1):
            pl.semaphore_signal(
                barrier,
                inc=1,
                device_id={"expert": z * 8 + (y + i) % 8, "tensor": which},
                device_id_type=MESH,
            )
            pl.semaphore_signal(
                barrier,
                inc=1,
                device_id={"expert": ((z + i) % 8) * 8 + y, "tensor": which},
                device_id_type=MESH,
            )

    ow_parts = [
        pltpu.make_async_copy(
            ow_hbm.at[:, pl.ds(n * 512, 512)], ow.at[:, pl.ds(n * 512, 512)], load_sem.at[6 + n]
        )
        for n in range(4)
    ]
    loads = [
        pltpu.make_async_copy(attn_hbm, attn, load_sem.at[0]),
        pltpu.make_async_copy(qw_hbm, qw.at[b, a, :, pl.ds(0, 512)], load_sem.at[1]),
        pltpu.make_async_copy(kvw_hbm, qw.at[b, a, :, pl.ds(512, 128)], load_sem.at[2]),
        pltpu.make_async_copy(wg_hbm.at[0], gate_up.at[0], load_sem.at[3]),
        pltpu.make_async_copy(wu_hbm.at[0], gate_up.at[2], load_sem.at[4]),
        pltpu.make_async_copy(wd_hbm.at[0], wd_own, load_sem.at[5]),
    ]
    loads[0].start()
    for part in ow_parts:
        part.start()
    for load in loads[1:]:
        load.start()

    loads[0].wait()
    for n in range(4):
        ow_parts[n].wait()
        cols = slice(n * 512, n * 512 + 512)
        partial[:, :, cols] = dot(attn[...], ow[:, cols]).astype(BF).reshape(8, TOKENS, 512)

    pl.semaphore_wait(barrier, 35)

    for k in range(4):
        theirs = 2 * k + 1 - core
        send(partial.at[theirs], mates.at[k], mate_send.at[k], mate_recv.at[k], e, partner)

    def chip_sum(k):
        arrived(mates.at[k], mate_send.at[k], mate_recv.at[k])
        return (partial[2 * k + core].astype(F32) + mates[k].astype(F32)).astype(BF)

    for i in (2, 1, 3):
        k = (chip + i) % 4
        sums_of_chip[k] = chip_sum(k)
        send(sums_of_chip.at[k], rs_in.at[chip], rs_send.at[k], rs_recv.at[chip], e, 2 * k + core)
        expect("rs", rs_in.at[k], rs_send.at[k], rs_recv.at[k])
    rs_in[chip] = chip_sum(chip)

    loads[1].wait()
    loads[2].wait()

    @pl.loop(1, 8)
    def _(i):
        d = (a + step_of(i)) % 8
        remote(
            qw.at[b, a], qw.at[b, a], q1_send.at[d], q1_recv.at[a], at(d, b), t
        ).start()

    def q1_left():
        @pl.loop(1, 8)
        def _(i):
            n = (a + i) % 8
            left(qw.at[b, a], q1_send.at[n], q1_recv.at[n])

    sent.append(q1_left)

    loads[3].wait()
    loads[4].wait()
    for k in range(2):
        send(gate_up.at[2 * k], gate_up.at[2 * k + 1], pair_send.at[k], pair_recv.at[k], e, partner)
        expect("pair", gate_up.at[2 * k + 1], pair_send.at[k], pair_recv.at[k])

    position = iota((GROUP, 64), 1)
    p_first, p_second = position // 8, position % 8
    expert_of = 2 * at(p_first, p_second) + parity
    ids = ids_ref[...].T
    weights = rw_ref[...].T
    named = jnp.zeros((GROUP, 64), F32)
    weight_of = jnp.zeros((GROUP, 64), F32)
    for k in range(TOP):
        hit = expert_of == ids[:, k : k + 1]
        named += jnp.where(hit, 1.0, 0.0)
        weight_of += jnp.where(hit, weights[:, k : k + 1], 0.0)
    lower = jnp.where(iota((GROUP, GROUP), 1) < iota((GROUP, GROUP), 0), 1.0, 0.0).astype(BF)
    rank = dot(lower, named.astype(BF))
    code = (named * (rank + 1.0)).astype(BF)
    slot = iota((64, SLOTS), 1)
    start = iota((64, SLOTS), 0) * CAP
    spread = jnp.where((slot >= start) & (slot < start + CAP), 1.0, 0.0).astype(BF)
    wanted = (iota((GROUP, SLOTS), 1) % CAP + 1).astype(F32)
    chosen = dot(code, spread) == wanted
    high = weight_of.astype(BF)
    low = (weight_of - high.astype(F32)).astype(BF)
    mix_hi[...] = jnp.where(chosen, dot(high, spread), 0.0).astype(BF)
    mix_lo[...] = jnp.where(chosen, dot(low, spread), 0.0).astype(BF)
    pick[...] = jnp.where(chosen, 1.0, 0.0).T.astype(BF)

    after, before = at(a, (b + 1) % 8), at(a, (b + 7) % 8)

    def ring(step):
        rows = ((b + 8 - step) % 8, (b + step) % 8)
        if step == 3:
            pieces = (qw.at[rows[0], pl.ds(0, 4)], qw.at[rows[1], pl.ds(4, 4)])
        else:
            pieces = (qw.at[rows[0]], qw.at[rows[1]])
        return [
            remote(pieces[k], pieces[k], q2_send.at[step, k], q2_recv.at[step, k], (after, before)[k], t)
            for k in range(2)
        ]

    def ring_wait(step):
        rows = ((b + 7 - step) % 8, (b + 1 + step) % 8)
        if step == 3:
            pieces = (qw.at[rows[0], pl.ds(0, 4)], qw.at[rows[1], pl.ds(4, 4)])
        else:
            pieces = (qw.at[rows[0]], qw.at[rows[1]])
        for k in range(2):
            arrived(pieces[k], q2_send.at[step, k], q2_recv.at[step, k])

    @pl.loop(1, 8)
    def _(i):
        s = (a + i) % 8
        arrived(qw.at[b, s], q1_send.at[s], q1_recv.at[s])

    def ring_start(step):
        for c in ring(step):
            c.start()
        sent.append(lambda: [c.wait_send() for c in ring(step)])
        coming["ring"] = [lambda: ring_wait(step)]

    ring_start(0)

    take("rs")

    total = res_ref[...].astype(F32)
    attn_sum = rs_in[0].astype(F32)
    for k in range(1, 4):
        attn_sum += rs_in[k].astype(F32)
    first_residual = (total + attn_sum).astype(BF)
    first[...] = first_residual
    normed = normalize(first_residual.astype(F32), attn_gain[...]).astype(BF)
    for s in range(4):
        normed_out[s] = normed[:, s * QUARTER : s * QUARTER + QUARTER]
    normed_in[t] = normed_out[t % 4]

    to_tensor("nb", lambda d: normed_out.at[d % 4], normed_in, nb_send, nb_recv)

    loads[5].wait()
    own_half = pl.ds(pl.multiple_of(side * 1024, 1024), 1024)
    other_half = pl.ds(pl.multiple_of((1 - side) * 1024, 1024), 1024)
    send(wd_own.at[:, own_half], wd.at[1], wd_send.at[0], wd_recv.at[0], e, partner)
    expect("wd", wd.at[1], wd_send.at[0], wd_recv.at[0])
    send(wd_own.at[:, other_half], wd.at[2], wd_send.at[1], wd_recv.at[1], e, cross)
    expect("wd cross", wd.at[2], wd_send.at[1], wd_recv.at[1])
    wd[0] = wd_own[:, own_half]

    take("nb")

    group = normed_in[...].reshape(GROUP, QUARTER)

    def gone_d2():
        @pl.when(core == 0)
        def _():
            left(r1.at[0, pl.ds(0, 7)], d2_send, d2_recv0.at[0, 0])

            @pl.when(half == 1)
            def _():
                left(r1.at[0, 0], d2_send, d2_recv0.at[0, 0])

        @pl.when(core == 1)
        def _():
            left(r1.at[0, pl.ds(0, 7)], d2_send, d2_recv0.at[0, 0])
            left(r1.at[0, 0, pl.ds(0, 4)], d2_send, d2_recv0.at[0, 0])

    def dispatch_first(p):
        for k in range(2):
            rows = slice(k * 384, k * 384 + 384)
            tx[p, 4 * k : 4 * k + 4] = (
                dot(pick[rows, :], group[:, p * PIECE : p * PIECE + PIECE])
                .astype(BF)
                .reshape(4, 8, 3, 4, PIECE)
            )

        @pl.loop(1, 8)
        def _(i):
            d = (a + step_of(i)) % 8
            remote(tx.at[p, d], r1.at[p, a], d1_send, d1_recv.at[p], at(d, b), t).start()

        pltpu.make_async_copy(tx.at[p, a], r1.at[p, a], d1_recv.at[p]).start()
        sent.append(lambda: left(tx.at[p, pl.ds(0, 7)], d1_send, d1_recv.at[p]))

    def dispatch_second(p):
        arrived(r1.at[p], d1_send, d1_recv.at[p])

        def core0_path(d):
            return r1.at[p, :, d], x0.at[p, z % 4], d2_recv0.at[p, z % 4]

        def core1_path(d, hf):
            return r1.at[p, pl.ds(4 * hf, 4), d], x1.at[p, y], d2_recv1.at[p, y]

        @pl.when(core == 0)
        def _():
            src, dst, sem = core0_path(b)

            @pl.when(half == 0)
            def _():
                pltpu.make_async_copy(src, dst, sem).start()

            @pl.when(half == 1)
            def _():
                remote(src, dst, d2_send, sem, e, core1).start()

            @pl.loop(1, 8)
            def _(i):
                d = (b + step_of(i)) % 8
                src, dst, sem = core0_path(d)
                remote(src, dst, d2_send, sem, at(a, d), core0 + half).start()

        @pl.when(core == 1)
        def _():
            src, dst, sem = core1_path(b, 0)
            remote(src, dst, d2_send, sem, e, core0).start()
            src, dst, sem = core1_path(b, 1)
            pltpu.make_async_copy(src, dst, sem).start()

            @pl.loop(1, 8)
            def _(i):
                d = (b + step_of(i)) % 8
                for hf in range(2):
                    src, dst, sem = core1_path(d, hf)
                    remote(src, dst, d2_send, sem, at(a, d), core0 + hf).start()

        sent.append(gone_d2)

    def forward0(p, k):
        arrived(x0.at[p, k], c_send, d2_recv0.at[p, k])
        remote(x0.at[p, k], c0.at[p, k], c_send, c_recv0.at[p, k], e, cross).start()

    def forward1(p, i):
        k = (y + step_of(i)) % 8
        arrived(x1.at[p, k], c_send, d2_recv1.at[p, k])
        remote(x1.at[p, k], c1.at[p, k], c_send, c_recv1.at[p, k], e, cross).start()

    def forward_rest(p):
        @pl.loop(0, 4)
        def _(i):
            forward0(p, i)

            @pl.when(i >= FIRST // 2)
            def _():
                forward1(p, 2 * i)
                forward1(p, 2 * i + 1)

        sent.append(lambda: (left(x0.at[p], c_send, c_recv0.at[p, 0]), left(x1.at[p], c_send, c_recv0.at[p, 0])))

    def forward_first(p):
        @pl.loop(0, FIRST)
        def _(i):
            forward1(p, i)

    def take_c0(p):
        @pl.loop(0, 4)
        def _(i):
            arrived(c0.at[p, i], c_send, c_recv0.at[p, i])

    def take_c1(p):
        @pl.loop(0, 8)
        def _(i):
            arrived(c1.at[p, i], c_send, c_recv1.at[p, i])

    def multiply(values, column, zero=False):
        rows = pl.ds(pl.multiple_of(column, PIECE), PIECE)
        for n in range(2):
            cols = slice(n * PAIR_HIDDEN, n * PAIR_HIDDEN + PAIR_HIDDEN)
            product = lax.dot_general(
                values,
                gate_up[2 * n : 2 * n + 2, :, rows].reshape(PAIR_HIDDEN, PIECE),
                (((1,), (1,)), ((), ())),
                preferred_element_type=F32,
            )
            hidden[:, cols] = product if zero else hidden[:, cols] + product

    def natural(ref, p):
        return ref[p].reshape(ROWS, PIECE)

    def turned(ref, p):
        return jnp.concatenate([ref[p, :, k].reshape(96, PIECE) for k in range(4)], axis=0)

    own, other = side * 1024, (1 - side) * 1024

    dispatch_first(0)
    dispatch_first(1)
    take("pair")
    take("wd cross")
    send(wd.at[2], wd.at[3], wd_send.at[2], wd_recv.at[2], e, partner)
    expect("wd", wd.at[3], wd_send.at[2], wd_recv.at[2])
    dispatch_second(0)
    forward_first(0)
    dispatch_second(1)
    forward_rest(0)
    multiply(natural(x0, 0), own, True)
    multiply(turned(x1, 0), own + QUARTER)
    forward_first(1)
    forward_rest(1)
    take("ring")
    ring_start(1)
    multiply(natural(x0, 1), own + PIECE)
    multiply(turned(x1, 1), own + QUARTER + PIECE)
    take_c0(0)
    multiply(natural(c0, 0), other)
    take_c1(0)
    multiply(turned(c1, 0), other + QUARTER)
    take_c0(1)
    multiply(natural(c0, 1), other + PIECE)
    take_c1(1)
    multiply(turned(c1, 1), other + QUARTER + PIECE)

    for r in range(2):
        rows = slice(r * 192, r * 192 + 192)
        gate = hidden[rows, 0:PAIR_HIDDEN]
        act[rows, :] = (
            gate * (1.0 / (1.0 + jnp.exp(-gate))) * hidden[rows, PAIR_HIDDEN : 2 * PAIR_HIDDEN]
        ).astype(BF)
        part = pl.ds(r * 192, 192)
        send(act.at[part], act_in.at[part], act_send.at[r], act_recv.at[r], e, cross)
    take("ring")
    ring_start(2)

    take("wd")
    for n in range(4):
        cols = slice(n * 256, n * 256 + 256)
        y_acc[:, cols] = dot(act[...], wd[0:2, :, cols].reshape(PAIR_HIDDEN, 256))

    first_zone = 4 * core

    def gone_r3():
        left(y1.at[0, pl.ds(0, 7)], r3_send, r3_recv.at[0])

        @pl.when((core == 0) & (half == 0))
        def _():
            left(y0.at[0, pl.ds(0, 3)], r3_send, r3_recv.at[0])
            left(y1.at[0, 0], r3_send, r3_recv.at[0])

        @pl.when((core == 0) & (half == 1))
        def _():
            left(y0.at[0], r3_send, r3_recv.at[0])
            left(y1.at[0, 0], r3_send, r3_recv.at[0])

        @pl.when(core == 1)
        def _():
            left(y0.at[0], r3_send, r3_recv.at[0])

    for r in range(2):
        rows = slice(r * 192, r * 192 + 192)
        zones = slice(2 * r, 2 * r + 2)
        arrived(act_in.at[pl.ds(r * 192, 192)], act_send.at[r], act_recv.at[r])
        for p in range(2):
            for n in (p, 2 + p):
                cols = slice(n * PIECE, n * PIECE + PIECE)
                out = y_acc[rows, cols] + dot(
                    act_in[rows, :], wd[2:4, :, cols].reshape(PAIR_HIDDEN, PIECE)
                )
                blocks = out.astype(BF).reshape(2, 8, 3, 4, PIECE)
                if n < 2:
                    y0[p, zones] = blocks
                else:
                    for k in range(2):
                        y1[p, :, 2 * r + k] = blocks[k]

            @pl.loop(2 * r, 2 * r + 2)
            def _(i):
                zone = first_zone + i
                src, dst = y0.at[p, i], r3.at[p, z]

                @pl.when(zone != z)
                def _():
                    remote(src, dst, r3_send, r3_recv.at[p], zone * 8 + y, core0).start()

                @pl.when((zone == z) & (core == 0))
                def _():
                    pltpu.make_async_copy(src, dst, r3_recv.at[p]).start()

                @pl.when((zone == z) & (core == 1))
                def _():
                    remote(src, dst, r3_send, r3_recv.at[p], e, core0).start()

            into = r3.at[p, y, pl.ds(first_zone + 2 * r, 2)]
            part = pl.ds(2 * r, 2)

            @pl.loop(1, 8)
            def _(i):
                d = (y + step_of(i)) % 8
                remote(
                    y1.at[p, d, part], into, r3_send, r3_recv.at[p], z * 8 + d, core1
                ).start()

            @pl.when(core == 1)
            def _():
                pltpu.make_async_copy(y1.at[p, y, part], into, r3_recv.at[p]).start()

            @pl.when(core == 0)
            def _():
                remote(y1.at[p, y, part], into, r3_send, r3_recv.at[p], e, core1).start()

    for p in range(2):
        sent.append(gone_r3)

    for p in range(2):
        arrived(r3.at[p], r3_send, r3_recv.at[p])

        @pl.loop(1, 8)
        def _(i):
            d = (a + step_of(i)) % 8
            remote(r3.at[p, :, d], r4.at[p, a], r4_send, r4_recv.at[p], at(d, b), t).start()

        pltpu.make_async_copy(r3.at[p, :, a], r4.at[p, a], r4_recv.at[p]).start()
        sent.append(lambda: left(r4.at[0, pl.ds(0, 7)], r4_send, r4_recv.at[0]))

    for p in range(2):
        arrived(r4.at[p], r4_send, r4_recv.at[p])
        returned = r4[p].reshape(SLOTS, PIECE)
        weighted = dot(mix_hi[...], returned) + dot(mix_lo[...], returned)
        sums_out[:, :, p * PIECE : p * PIECE + PIECE] = weighted.astype(BF).reshape(
            8, TOKENS, PIECE
        )
    sums_in[t] = sums_out[t]

    to_tensor("sums", lambda d: sums_out.at[d], sums_in, sums_send, sums_recv)
    take("ring")
    ring_start(3)
    take("sums")

    expert_sum = jnp.concatenate(
        [sums_in[s].astype(F32) + sums_in[s + 4].astype(F32) for s in range(4)], axis=1
    )
    next_residual = (first[...].astype(F32) + expert_sum).astype(BF)
    moved_ref[...] = next_residual
    nx[t] = normalize(next_residual.astype(F32), input_gain[...]).astype(BF)

    for i in (2, 1, 3):
        d = 2 * ((chip + i) % 4) + core
        send(nx.at[t], nx.at[t], nx_send.at[i], nx_recv.at[t], e, d)
    send(nx.at[t], nx.at[t], nx_send.at[0], nx_recv.at[t], e, partner)
    for i in (1, 3, 2):
        s = 2 * ((chip + i) % 4) + core
        arrived(nx.at[s], nx_send.at[i], nx_recv.at[s])
        send(nx.at[s], nx.at[s], nx_send.at[4 + i], nx_recv.at[s], e, partner)

    take("ring")

    for i in range(4):
        s = 2 * ((chip + i) % 4) + 1 - core
        arrived(nx.at[s], nx_send.at[i], nx_recv.at[s])

    tokens = nx[...].reshape(GROUP, D)
    raw = jnp.zeros((GROUP, QKV), F32)
    for zz in range(8):
        blocks = []
        for yy in range(8):
            second = zz + core * (yy - zz)
            blocks.append(qw[second, yy + core * (zz - yy)])
        raw += dot(tokens[:, zz * 256 : zz * 256 + 256], jnp.concatenate(blocks, axis=0))
    raw_ref[...] = raw

    for gone in sent:
        gone()


def finish(moved_ref, raw_ref, q_gain, k_gain, next_ref, queries_ref, kv_ref):
    t = lax.axis_index("tensor")
    next_ref[...] = moved_ref[...]
    for head in range(4):
        cols = slice(head * HEAD, head * HEAD + HEAD)
        queries_ref[:, cols] = normalize(raw_ref[:, cols], q_gain[...]).astype(BF)
    kv_raw = raw_ref[:, 512:QKV]
    kv_ref[...] = jnp.where(t < KV_HEADS, normalize(kv_raw, k_gain[...]), kv_raw).astype(BF)


def per_device(
    attn_out,
    out_weight,
    residual,
    attn_gain,
    expert_ids,
    route_weights,
    w_gate,
    w_up,
    w_down,
    input_gain,
    q_weight,
    kv_weight,
    q_gain,
    k_gain,
):
    any_spec = pl.BlockSpec(memory_space=pl.ANY)
    vmem = pl.BlockSpec(memory_space=pltpu.VMEM)
    dma = pltpu.SemaphoreType.DMA
    rows = (3, 4, PIECE)

    def buf(*shape):
        return pltpu.VMEM(shape, BF)

    moved, raw = pl.pallas_call(
        kernel,
        out_shape=(
            jax.ShapeDtypeStruct((TOKENS, D), BF),
            jax.ShapeDtypeStruct((GROUP, QKV), F32),
        ),
        in_specs=[
            any_spec,
            any_spec,
            vmem,
            vmem,
            vmem,
            vmem,
            any_spec,
            any_spec,
            any_spec,
            vmem,
            any_spec,
            any_spec,
        ],
        out_specs=(vmem, vmem),
        scratch_shapes=[
            buf(GROUP, 512),
            buf(512, D),
            buf(4, HIDDEN, D),
            buf(HIDDEN, D),
            buf(4, HIDDEN, D // 2),
            buf(8, 8, 32, QKV),
            buf(8, TOKENS, D),
            buf(4, TOKENS, D),
            buf(4, TOKENS, D),
            buf(4, TOKENS, D),
            buf(4, TOKENS, QUARTER),
            buf(8, TOKENS, QUARTER),
            buf(SLOTS, GROUP),
            buf(GROUP, SLOTS),
            buf(GROUP, SLOTS),
            buf(2, 8, 8, *rows),
            buf(2, 8, 8, *rows),
            buf(2, 4, 8, *rows),
            buf(2, 8, 4, *rows),
            buf(2, 4, 8, *rows),
            buf(2, 8, 4, *rows),
            pltpu.VMEM((ROWS, 2 * PAIR_HIDDEN), F32),
            buf(ROWS, PAIR_HIDDEN),
            buf(ROWS, PAIR_HIDDEN),
            pltpu.VMEM((ROWS, D // 2), F32),
            buf(2, 4, 8, *rows),
            buf(2, 8, 4, *rows),
            buf(2, 8, 8, *rows),
            buf(2, 8, 8, *rows),
            buf(8, TOKENS, QUARTER),
            buf(8, TOKENS, QUARTER),
            buf(TOKENS, D),
            buf(8, TOKENS, D),
            dma((10,)),
            dma((4,)),
            dma((4,)),
            dma((4,)),
            dma((4,)),
            dma((8,)),
            dma((8,)),
            dma((2,)),
            dma((2,)),
            dma((3,)),
            dma((3,)),
            dma((8,)),
            dma((8,)),
            dma((4, 2)),
            dma((4, 2)),
            dma,
            dma((2,)),
            dma,
            dma((2, 4)),
            dma((2, 8)),
            dma,
            dma((2, 4)),
            dma((2, 8)),
            dma((2,)),
            dma((2,)),
            dma,
            dma((2,)),
            dma,
            dma((2,)),
            dma((8,)),
            dma((8,)),
            dma((8,)),
            dma((8,)),
        ],
        compiler_params=pltpu.CompilerParams(
            collective_id=0, has_side_effects=True, vmem_limit_bytes=66_400_000
        ),
    )(
        attn_out,
        out_weight,
        residual,
        attn_gain.reshape(1, -1),
        expert_ids.T,
        route_weights.T,
        jnp.swapaxes(w_gate, 1, 2),
        jnp.swapaxes(w_up, 1, 2),
        w_down,
        input_gain.reshape(1, -1),
        q_weight,
        kv_weight,
    )
    return pl.pallas_call(
        finish,
        out_shape=(
            jax.ShapeDtypeStruct((TOKENS, D), BF),
            jax.ShapeDtypeStruct((GROUP, 512), BF),
            jax.ShapeDtypeStruct((GROUP, HEAD), BF),
        ),
        in_specs=[vmem] * 4,
        out_specs=(vmem, vmem, vmem),
        compiler_params=pltpu.CompilerParams(vmem_limit_bytes=66_400_000),
    )(moved, raw, q_gain.reshape(1, -1), k_gain.reshape(1, -1))


def solution(mesh):
    return jax.shard_map(
        per_device,
        mesh=mesh,
        in_specs=(
            P("expert", "tensor"),
            P("tensor", None),
            P(("expert", "tensor"), None),
            P(),
            P("expert", None),
            P("expert", None),
            P("expert", None, "tensor"),
            P("expert", None, "tensor"),
            P("expert", "tensor", None),
            P(),
            P("expert", "tensor"),
            P("expert", "tensor"),
            P(),
            P(),
        ),
        out_specs=(P(("expert", "tensor"), None), P("expert", "tensor"), P("expert", "tensor")),
        check_vma=False,
    )
```
